32 devices in a mesh: series: 2 (over y), ta: 4 (over z), pb: 4 (over x, core).
Axes of the slice: x: 2, y: 2, z: 4, core: 2. Of those that a mesh axis runs over, the one named last changes fastest.
Arguments:
- blocks: bfloat16 [8, 4, 4, 32, 128, 128], P(('series', 'ta'), 'pb'), parts along dimension 0, may hold values from -6 to 6
- qz_factor: bfloat16 [2048, 256], P(('series', 'ta')), parts along dimension 0, may hold values from -0.5 to 0.5
- qy_factor: bfloat16 [2048, 256], P(('series', 'ta')), parts along dimension 0, may hold values from -0.5 to 0.5
- block_owner: int32 [8, 4, 4], P(('series', 'ta'), 'pb'), parts along dimension 0, may hold values from -1 to 3, as said below
- block_cells: int32 [8, 4, 4, 2], P(('series', 'ta'), 'pb'), parts along dimension 0, may hold values from 0 to 7, as said below
Outputs:
- frame_factor: float32 [1024, 256], P(('series', 'ta', 'pb')), parts along dimension 0
- slot_misfit: float32 [8, 4, 4], P(('series', 'ta'), 'pb'), parts along dimension 0
The draws below stay inside these ranges and needn't reach their ends.
There are 2 independent parts, one for each index of `series`. The reference program is written for one: setup_inputs(seed, part) draws one part's arguments, and reference() takes and returns one part's arrays. A program takes and returns all parts, laid end to end along the dimension named above; each array names one. Nothing has to cross between parts.
Inputs may be any that keep to these rules, and one draw needn't show every extreme that they name: `block_owner`: the slots of device index p along pb hold only frame blocks u * 4 + p. No two live slots of one frame block share the same pair of cells. Every frame block has at least one live slot, and some slot is empty. `block_cells`: each entry is a block index below 8.
All inputs are finite; a program needn't handle non-finite values.
Results may differ from the reference program's by a relative error of at most 0.0003.
Values may be sent and summed in bfloat16 or wider, within the bound.
No kernel may reach another device: no remote copies, remote signals or barrier semaphores. Data moves between devices by JAX's collectives and lax.ppermute only.
A program may use at most 64 MiB of HBM per device.

```python
import jax
import jax.numpy as jnp
from jax import lax

R = 256
Q = 1024
QB = 128
FB = 32
NB = 4
FRAMES = 512
N_TA = 4
N_PB = 4


def slot_layout(key):
    cell_total = Q // QB * (Q // QB)

    def column_draw(column):
        column_key = jax.random.fold_in(jax.random.fold_in(key, 7001), column)
        shuffled = jax.random.permutation(column_key, N_TA * NB).reshape(N_TA, NB)
        slot_owner = shuffled % N_TA
        rank_index = shuffled // N_TA
        cell_keys = jax.random.split(jax.random.fold_in(column_key, 5), N_TA)
        tables = jax.vmap(lambda one_key: jax.random.permutation(one_key, cell_total))(cell_keys)
        slot_cell = tables[slot_owner, rank_index]
        coin_flip = jax.random.randint(jax.random.fold_in(column_key, 9), (N_TA, NB), 0, 4)
        random_live = jnp.where(coin_flip > 0, 1, 0)
        forced_dead = jnp.where((rank_index == NB - 1) & (slot_owner == 0), 0, random_live)
        live_flag = jnp.where(rank_index == 0, 1, forced_dead)
        return (jnp.where(live_flag == 1, slot_owner, -1), slot_cell)
    owners, cells = jax.vmap(column_draw)(jnp.arange(N_PB))
    return (jnp.transpose(owners, (1, 0, 2)).astype(jnp.int32), jnp.transpose(cells, (1, 0, 2)).astype(jnp.int32))


def draw_block_owner(key, part):
    owners, cells = slot_layout(key)
    return owners


def draw_block_cells(key, part):
    owners, cells = slot_layout(key)
    grid_side = Q // QB
    return jnp.stack([cells // grid_side, cells % grid_side], axis=-1).astype(jnp.int32)


def shard_levels(stream_key, shape, cuts, least, high):
    level, own = 1.0, jax.random.fold_in(stream_key, 6)
    for axis_at, shards_of in cuts:
        heights = jnp.exp(jax.random.uniform(jax.random.fold_in(own, axis_at), (shards_of,), jnp.float32, least / len(cuts), high / len(cuts)))
        level = level * jnp.repeat(heights, shape[axis_at] // shards_of).reshape([-1 if axis == axis_at else 1 for axis in range(len(shape))])
    return level


def noise(own_key, shape, scale, most, cuts=(), kind=jnp.bfloat16):
    values = scale * jax.random.normal(own_key, shape, jnp.float32)
    if cuts:
        values = values * shard_levels(own_key, shape, cuts, -0.22, 0.18)
    return jnp.clip(values, -most, most).astype(kind)


def setup_inputs(seed: int = 0, part: int = 0) -> dict:
    splits = jax.random.split(jax.random.key(seed), 6)
    own_keys = jax.random.split(jax.random.fold_in(splits[5], part), 6)
    return {
        "blocks": noise(own_keys[0], (N_TA, N_PB, NB, FB, QB, QB), 1.0, 6.0, ((0, 4), (1, 4))),
        "qz_factor": noise(own_keys[1], (Q, R), QB ** -0.5, 0.5, ((0, 4),)),
        "qy_factor": noise(own_keys[2], (Q, R), QB ** -0.5, 0.5, ((0, 4),)),
        "block_owner": draw_block_owner(jax.random.fold_in(jax.random.fold_in(splits[5], part), 71), part),
        "block_cells": draw_block_cells(jax.random.fold_in(jax.random.fold_in(splits[5], part), 71), part),
    }


ridge_weight = 0.1
top_precision = lax.Precision.HIGHEST

def solve_rows(rhs_rows, system):
    lower_factor = jnp.linalg.cholesky(system)
    halfway = lax.linalg.triangular_solve(lower_factor, rhs_rows, left_side=False, lower=True, transpose_a=True)
    return lax.linalg.triangular_solve(lower_factor, halfway, left_side=False, lower=True, transpose_a=False)

def reference(blocks, qz_factor, qy_factor, block_owner, block_cells):
    grid_side = Q // QB
    slot_count = N_TA * N_PB * NB
    block_count = N_TA * N_PB
    cube_data = blocks.reshape(slot_count, FB, QB, QB)
    slot_owner = block_owner.reshape(slot_count)
    slot_cells = block_cells.reshape(slot_count, 2)
    column = (jnp.arange(slot_count) // NB % N_PB).astype(jnp.int32)
    live_flag = (slot_owner >= 0).astype(jnp.float32)
    frame_block = jnp.where(slot_owner >= 0, slot_owner * N_PB + column, 0).astype(jnp.int32)
    qz_panels = qz_factor.astype(jnp.float32).reshape(grid_side, QB, R)
    qy_panels = qy_factor.astype(jnp.float32).reshape(grid_side, QB, R)
    gram_z = jnp.einsum('azr,azs->ars', qz_panels, qz_panels, precision=top_precision)
    gram_y = jnp.einsum('azr,azs->ars', qy_panels, qy_panels, precision=top_precision)

    def accumulate(running, slot_item):
        totals, tallies = running
        cube_one, qz_cell, qy_cell, block_id, flag_one = slot_item
        panel_z = lax.dynamic_index_in_dim(qz_panels, qz_cell, 0, keepdims=False)
        panel_y = lax.dynamic_index_in_dim(qy_panels, qy_cell, 0, keepdims=False)
        inner_sum = jnp.einsum('fzy,yr->fzr', cube_one.astype(jnp.float32), panel_y, precision=top_precision)
        contribution = jnp.sum(inner_sum * panel_z[None], axis=1) * flag_one
        current = lax.dynamic_slice_in_dim(totals, block_id * FB, FB, 0)
        totals = lax.dynamic_update_slice_in_dim(totals, current + contribution, block_id * FB, 0)
        tallies = tallies.at[block_id, qz_cell * grid_side + qy_cell].add(flag_one)
        return ((totals, tallies), None)
    start_state = (jnp.zeros((FRAMES, R), jnp.float32), jnp.zeros((block_count, grid_side * grid_side), jnp.float32))
    (totals, tallies), _ = lax.scan(accumulate, start_state, (cube_data, slot_cells[:, 0], slot_cells[:, 1], frame_block, live_flag))

    def solve_block(block_item):
        rhs_rows, tally_row = block_item
        weights = tally_row.reshape(grid_side, grid_side)
        mixture = jnp.einsum('ab,brs->ars', weights, gram_y, precision=top_precision)
        system = jnp.sum(gram_z * mixture, axis=0) + ridge_weight * jnp.eye(R, dtype=jnp.float32)
        return solve_rows(rhs_rows, system)
    frame_factor = lax.map(solve_block, (totals.reshape(block_count, FB, R), tallies)).reshape(FRAMES, R)
    frame_low = frame_factor.astype(jnp.bfloat16)

    def misfit_one(slot_item):
        cube_one, qz_cell, qy_cell, block_id, flag_one = slot_item
        panel_z = lax.dynamic_index_in_dim(qz_panels, qz_cell, 0, keepdims=False)
        panel_y = lax.dynamic_index_in_dim(qy_panels, qy_cell, 0, keepdims=False)
        rows_low = lax.dynamic_slice_in_dim(frame_low, block_id * FB, FB, 0).astype(jnp.float32)
        outer_prod = (rows_low[:, None, :] * panel_z[None]).astype(jnp.bfloat16)
        model = jnp.einsum('fzr,yr->fzy', outer_prod.astype(jnp.float32), panel_y, precision=top_precision)
        deviation = cube_one.astype(jnp.float32) - model
        return jnp.sum(deviation * deviation) / (FB * QB * QB) * flag_one
    slot_misfit = lax.map(misfit_one, (cube_data, slot_cells[:, 0], slot_cells[:, 1], frame_block, live_flag))
    return (frame_factor, slot_misfit.reshape(N_TA, N_PB, NB))
```

```python
import functools

import jax
import jax.numpy as jnp
from jax import lax
from jax.experimental import pallas as pl
from jax.experimental.pallas import tpu as pltpu
from jax.sharding import PartitionSpec as P

ridge_weight = 0.1
info_rows = 16
ring_limit = 8
newton_steps = 10
newton_goal = 4e-4
top = lax.Precision.HIGHEST
f32 = jnp.float32
bf16 = jnp.bfloat16

vmem_spec = pl.BlockSpec(memory_space=pltpu.VMEM)
smem_spec = pl.BlockSpec(memory_space=pltpu.SMEM)
any_spec = pl.BlockSpec(memory_space=pl.ANY)


def params(mib):
    return pltpu.CompilerParams(vmem_limit_bytes=mib * 1024 * 1024)


def pack_kernel(place, owner, cells, z_ref, y_ref, out_ref):
    half = z_ref.shape[0] // 2
    slots = owner.shape[0]
    start = pl.multiple_of(place[2] * half, half)
    out_ref[0:half, :] = z_ref[pl.ds(start, half), :]
    out_ref[half : 2 * half, :] = y_ref[pl.ds(start, half), :]
    shape = (info_rows, z_ref.shape[1])
    row = lax.broadcasted_iota(jnp.int32, shape, 0)
    lane = lax.broadcasted_iota(jnp.int32, shape, 1)
    table = jnp.zeros(shape, jnp.int32)
    for s in range(slots):
        for r, value in enumerate((owner[s] + 1, cells[2 * s], cells[2 * s + 1])):
            table = jnp.where((row == r) & (lane == s), value, table)
    out_ref[2 * half :, :] = table.astype(f32).astype(bf16)


def term_kernel(
    ta_count, edge, place, owner, cells, x_ref, z_ref, y_ref, far_ref, pair_ref, blocks,
    terms, full_z, full_y, info, cube, sems,
):
    slots, frames = cube.shape[0], cube.shape[1]
    rows = z_ref.shape[0]
    half = rows // 2
    piece = 2 * half + info_rows
    copies = [pltpu.make_async_copy(blocks.at[0, 0, s], cube.at[s], sems.at[s]) for s in range(slots)]
    for copy in copies:
        copy.start()
    me, parity = place[0], place[2]
    mine = pl.multiple_of(me * rows, rows)
    full_z[pl.ds(mine, rows), :] = z_ref[...]
    full_y[pl.ds(mine, rows), :] = y_ref[...]
    info[0:info_rows, :] = x_ref[2 * half :, :]
    for k in range(1, ta_count):
        base = (k - 1) * piece
        source = lax.rem(me + (ta_count - k), ta_count) * rows
        here = pl.multiple_of(source + parity * half, half)
        there = pl.multiple_of(source + (1 - parity) * half, half)
        full_z[pl.ds(here, half), :] = far_ref[base : base + half, :]
        full_y[pl.ds(here, half), :] = far_ref[base + half : base + 2 * half, :]
        full_z[pl.ds(there, half), :] = pair_ref[base : base + half, :]
        full_y[pl.ds(there, half), :] = pair_ref[base + half : base + 2 * half, :]
        info[k * info_rows : (k + 1) * info_rows, :] = far_ref[base + 2 * half : base + piece, :]
    terms[...] = jnp.zeros_like(terms)
    chunk = 8
    rank = full_z.shape[1]
    for s in range(slots):
        copies[s].wait()
        panel_z = full_z[pl.ds(pl.multiple_of(cells[2 * s] * edge, edge), edge), :].astype(f32)
        panel_y = full_y[pl.ds(pl.multiple_of(cells[2 * s + 1] * edge, edge), edge), :]
        u = owner[s]
        live = u >= 0
        k = lax.rem(jnp.maximum(u, 0) + (ta_count - me), ta_count)
        for f in range(0, frames, chunk):
            part = cube[s, f : f + chunk].reshape(chunk * edge, edge)
            inner = jnp.dot(part, panel_y, preferred_element_type=f32)
            summed = jnp.sum(inner.reshape(chunk, edge, rank) * panel_z[None], axis=1)
            at = pl.ds(pl.multiple_of(k * frames + f, chunk), chunk)
            terms[at, :] += jnp.where(live, summed, 0.0)


def system_kernel(ta_count, slots, edge, place, info, full_z, full_y, system, inverse, codes):
    rank = full_z.shape[1]
    grid = full_z.shape[0] // edge
    me = place[0]
    lane = lax.broadcasted_iota(jnp.int32, (1, rank), 1)
    for k in range(ta_count):
        table = info[k * info_rows : (k + 1) * info_rows, :].astype(f32)
        cell = (table[1:2, :] * grid + table[2:3, :]).astype(jnp.int32)
        wanted = table[0:1, :].astype(jnp.int32) == me + 1
        code = jnp.where(wanted, cell, -1)
        for s in range(slots):
            codes[k * slots + s] = jnp.max(jnp.where(lane == s, code, -1))
    eye = lax.broadcasted_iota(jnp.int32, (rank, rank), 0) == lax.broadcasted_iota(
        jnp.int32, (rank, rank), 1
    )
    system[...] = jnp.where(eye, ridge_weight, 0.0).astype(f32)

    @pl.loop(0, ta_count * slots)
    def _(i):
        code = codes[i]

        @pl.when(code >= 0)
        def _():
            at = pl.multiple_of(lax.div(code, grid) * edge, edge)
            panel_z = full_z[pl.ds(at, edge), :]
            at = pl.multiple_of(lax.rem(code, grid) * edge, edge)
            panel_y = full_y[pl.ds(at, edge), :]
            over = (((0,), (0,)), ((), ()))
            gram_z = lax.dot_general(panel_z, panel_z, over, preferred_element_type=f32)
            gram_y = lax.dot_general(panel_y, panel_y, over, preferred_element_type=f32)
            system[...] += gram_z * gram_y

    matrix = system[...]
    down = 1.0 / jnp.sum(jnp.where(eye, matrix, 0.0), axis=1, keepdims=True)
    across = 1.0 / jnp.sum(jnp.where(eye, matrix, 0.0), axis=0, keepdims=True)
    inverse[...] = jnp.where(eye, 2.0 * across, 0.0) - down * matrix * across

    def going(state):
        step, error = state
        return (step < newton_steps) & jnp.logical_not(error <= newton_goal)

    def newton(state):
        guess = inverse[...]
        miss = jnp.where(eye, 1.0, 0.0) - jnp.dot(
            system[...], guess, precision=top, preferred_element_type=f32
        )
        inverse[...] = guess + jnp.dot(guess, miss, precision=top, preferred_element_type=f32)
        return state[0] + 1, jnp.sum(miss * miss)

    _, error = lax.while_loop(going, newton, (jnp.int32(0), jnp.float32(jnp.inf)))

    @pl.when(jnp.logical_not(error <= newton_goal))
    def _():
        inverse[...] = system[...]
        lanes = lax.broadcasted_iota(jnp.int32, (1, rank), 1)
        subs = lax.broadcasted_iota(jnp.int32, (rank, 1), 0)

        @pl.loop(0, rank)
        def _(k):
            whole = inverse[...]
            row = inverse[pl.ds(k, 1), :]
            column = jnp.sum(jnp.where(lanes == k, whole, 0.0), axis=1, keepdims=True)
            pivot = 1.0 / jnp.sum(jnp.where(lanes == k, row, 0.0), axis=1, keepdims=True)
            scaled = jnp.where(lanes == k, 1.0, row) * pivot
            rest = jnp.where(lanes == k, 0.0, whole) - column * scaled
            inverse[...] = jnp.where(subs == k, scaled, rest)


def solve_kernel(ta_count, own, far, system, inverse, rows_out, low_out):
    frames = rows_out.shape[0]
    rhs = own[0:frames, :]
    for k in range(1, ta_count):
        rhs = rhs + far[(k - 1) * frames : k * frames, :]
    dot = functools.partial(jnp.dot, precision=top, preferred_element_type=f32)
    rows = dot(rhs, inverse[...])
    rest = rhs - dot(rows, system[...])
    rows = rows + dot(rest, inverse[...])
    rows_out[...] = rows
    low_out[...] = rows.astype(bf16)


def misfit_kernel(
    ta_count, edge, place, owner, cells, low, far, full_z, full_y, blocks, out, cube, every, sems
):
    slots, frames = cube.shape[0], cube.shape[1]
    copies = [pltpu.make_async_copy(blocks.at[0, 0, s], cube.at[s], sems.at[s]) for s in range(slots)]
    for copy in copies:
        copy.start()
    every[0] = low[...].astype(f32)
    for k in range(1, ta_count):
        every[k] = far[(k - 1) * frames : k * frames, :].astype(f32)
    me = place[0]
    chunk = 8
    rank = full_z.shape[1]
    lane = lax.broadcasted_iota(jnp.int32, out.shape, 1)
    answer = jnp.zeros(out.shape, f32)
    over = (((1,), (1,)), ((), ()))
    for s in range(slots):
        copies[s].wait()
        panel_z = full_z[pl.ds(pl.multiple_of(cells[2 * s] * edge, edge), edge), :].astype(f32)
        panel_y = full_y[pl.ds(pl.multiple_of(cells[2 * s + 1] * edge, edge), edge), :]
        u = owner[s]
        k = lax.rem(me + (ta_count - jnp.maximum(u, 0)), ta_count)
        total = jnp.zeros((8, edge), f32)
        for f in range(0, frames, chunk):
            rows = every[k, f : f + chunk, :]
            outer = (rows[:, None, :] * panel_z[None]).astype(bf16).reshape(chunk * edge, rank)
            model = lax.dot_general(outer, panel_y, over, preferred_element_type=f32)
            off = cube[s, f : f + chunk].reshape(chunk * edge, edge).astype(f32) - model
            total = total + jnp.sum((off * off).reshape(chunk * edge // 8, 8, edge), axis=0)
        mean = jnp.sum(total) * (1.0 / (frames * edge * edge))
        answer = jnp.where((lane == s) & (u >= 0), mean, answer)
    out[...] = answer


def around(x, axis, count):
    if count <= ring_limit:
        turns = [
            lax.ppermute(x, axis, [(i, (i + k) % count) for i in range(count)])
            for k in range(1, count)
        ]
        return jnp.concatenate(turns, axis=0)
    every = lax.all_gather(x, axis, axis=0)
    order = (lax.axis_index(axis) - jnp.arange(1, count)) % count
    return every[order].reshape((count - 1) * x.shape[0], x.shape[1])


def deliver(terms, axis, count):
    frames = terms.shape[0] // count
    if count <= ring_limit:
        turns = [
            lax.ppermute(
                terms[k * frames : (k + 1) * frames],
                axis,
                [(i, (i + k) % count) for i in range(count)],
            )
            for k in range(1, count)
        ]
        return jnp.concatenate(turns, axis=0)
    me = lax.axis_index(axis)
    split = terms.reshape(count, frames, terms.shape[1])
    arrived = lax.all_to_all(
        split[(jnp.arange(count) - me) % count], axis, split_axis=0, concat_axis=0
    )
    order = (me - jnp.arange(1, count)) % count
    return arrived[order].reshape((count - 1) * frames, terms.shape[1])


def body(blocks, qz_factor, qy_factor, block_owner, block_cells):
    ta_count, pb_count = lax.axis_size("ta"), lax.axis_size("pb")
    slots, frames, edge = blocks.shape[2], blocks.shape[3], blocks.shape[4]
    rows, rank = qz_factor.shape
    half = rows // 2
    piece = 2 * half + info_rows
    me, column = lax.axis_index("ta"), lax.axis_index("pb")
    place = jnp.stack([me, column, column % 2]).astype(jnp.int32)
    owner = block_owner.reshape(slots)
    cells = block_cells.reshape(slots * 2)
    shape = jax.ShapeDtypeStruct
    packed = pl.pallas_call(
        pack_kernel,
        out_shape=shape((piece, rank), bf16),
        in_specs=[smem_spec] * 3 + [vmem_spec] * 2,
        out_specs=vmem_spec,
        compiler_params=params(4),
        name="pack",
    )(place, owner, cells, qz_factor, qy_factor)
    far = around(packed, "ta", ta_count)
    pair = lax.ppermute(far, "pb", [(i, i ^ 1) for i in range(pb_count)])
    terms, full_z, full_y, info = pl.pallas_call(
        functools.partial(term_kernel, ta_count, edge),
        out_shape=[
            shape((ta_count * frames, rank), f32),
            shape((ta_count * rows, rank), bf16),
            shape((ta_count * rows, rank), bf16),
            shape((ta_count * info_rows, rank), bf16),
        ],
        in_specs=[smem_spec] * 3 + [vmem_spec] * 5 + [any_spec],
        out_specs=[vmem_spec] * 4,
        scratch_shapes=[
            pltpu.VMEM((slots, frames, edge, edge), bf16),
            pltpu.SemaphoreType.DMA((slots,)),
        ],
        compiler_params=params(24),
        name="terms",
    )(place, owner, cells, packed, qz_factor, qy_factor, far, pair, blocks)
    arrived = deliver(terms, "ta", ta_count)
    system, inverse = pl.pallas_call(
        functools.partial(system_kernel, ta_count, slots, edge),
        out_shape=[shape((rank, rank), f32)] * 2,
        in_specs=[smem_spec] + [vmem_spec] * 3,
        out_specs=[vmem_spec] * 2,
        scratch_shapes=[pltpu.SMEM((ta_count * slots,), jnp.int32)],
        compiler_params=params(16),
        name="system",
    )(place, info, full_z, full_y)
    new_rows, low = pl.pallas_call(
        functools.partial(solve_kernel, ta_count),
        out_shape=[shape((frames, rank), f32), shape((frames, rank), bf16)],
        in_specs=[vmem_spec] * 4,
        out_specs=[vmem_spec] * 2,
        compiler_params=params(8),
        name="solve",
    )(terms, arrived, system, inverse)
    others = around(low, "ta", ta_count)
    misfit = pl.pallas_call(
        functools.partial(misfit_kernel, ta_count, edge),
        out_shape=shape((1, slots), f32),
        in_specs=[smem_spec] * 3 + [vmem_spec] * 4 + [any_spec],
        out_specs=vmem_spec,
        scratch_shapes=[
            pltpu.VMEM((slots, frames, edge, edge), bf16),
            pltpu.VMEM((ta_count, frames, rank), f32),
            pltpu.SemaphoreType.DMA((slots,)),
        ],
        compiler_params=params(24),
        name="misfit",
    )(place, owner, cells, low, others, full_z, full_y, blocks)
    return (new_rows, misfit.reshape(1, 1, slots))


def solution(mesh):
    placed = (
        P(("series", "ta"), "pb", None, None, None, None),
        P(("series", "ta"), None),
        P(("series", "ta"), None),
        P(("series", "ta"), "pb", None),
        P(("series", "ta"), "pb", None, None),
    )
    return jax.shard_map(
        body,
        mesh=mesh,
        in_specs=placed,
        out_specs=(P(("series", "ta", "pb"), None), P(("series", "ta"), "pb", None)),
        check_vma=False,
    )
```

```python
import functools

import jax
import jax.numpy as jnp
from jax import lax
from jax.experimental import pallas as pl
from jax.experimental.pallas import tpu as pltpu
from jax.sharding import PartitionSpec as P

ridge_weight = 0.1
info_rows = 16
ring_limit = 8
newton_steps = 10
newton_goal = 4e-4
top = lax.Precision.HIGHEST
f32 = jnp.float32
bf16 = jnp.bfloat16

vmem_spec = pl.BlockSpec(memory_space=pltpu.VMEM)
smem_spec = pl.BlockSpec(memory_space=pltpu.SMEM)
hbm_spec = pl.BlockSpec(memory_space=pltpu.HBM)


def held(x):
    return pltpu.with_memory_space_constraint(x, pltpu.HBM)


def params(mib):
    return pltpu.CompilerParams(vmem_limit_bytes=mib * 1024 * 1024)


def pack_kernel(owner, cells, z_hbm, y_hbm, out_ref, rest_ref, table_ref, sems):
    half = z_hbm.shape[0] // 2
    rank = z_hbm.shape[1]
    slots = owner.shape[2]
    parity = lax.rem(lax.axis_index("pb"), 2)
    copies = []
    for i, source in enumerate((z_hbm, y_hbm)):
        for j, target in enumerate((out_ref, rest_ref)):
            at = pl.multiple_of((parity if j == 0 else 1 - parity) * half, half)
            copies.append(
                pltpu.make_async_copy(
                    source.at[pl.ds(at, half), :],
                    target.at[i * half : (i + 1) * half, :],
                    sems.at[2 * i + j],
                )
            )
    for copy in copies:
        copy.start()
    shape = (info_rows, rank)
    row = lax.broadcasted_iota(jnp.int32, shape, 0)
    lane = lax.broadcasted_iota(jnp.int32, shape, 1)
    table = jnp.zeros(shape, jnp.int32)
    for s in range(slots):
        values = (owner[0, 0, s], cells[0, 0, 0, s], cells[0, 0, 1, s])
        for r, value in enumerate(values):
            table_ref[r * slots + s] = value
            shown = value + 1 if r == 0 else value
            table = jnp.where((row == r) & (lane == s), shown, table)
    out_ref[2 * half :, :] = table.astype(f32).astype(bf16)
    for copy in copies:
        copy.wait()


def load_kernel(blocks, cube, sems):
    slots = cube.shape[0]
    copies = [pltpu.make_async_copy(blocks.at[0, 0, s], cube.at[s], sems.at[s]) for s in range(slots)]
    for copy in copies:
        copy.start()
    for copy in copies:
        copy.wait()


def term_kernel(
    ta_count, edge, table, near_ref, rest_ref, far_ref, pair_ref, cube, terms, full_z, full_y, info
):
    slots, frames = cube.shape[0], cube.shape[1]
    half = rest_ref.shape[0] // 2
    piece = 2 * half + info_rows
    me = lax.axis_index("ta")
    parity = lax.rem(lax.axis_index("pb"), 2)
    for k in range(ta_count):
        base = (k - 1) * piece
        source = lax.rem(me + (ta_count - k), ta_count) * (2 * half)
        here = pl.multiple_of(source + parity * half, half)
        there = pl.multiple_of(source + (1 - parity) * half, half)
        one = near_ref if k == 0 else far_ref.at[base : base + piece, :]
        two = rest_ref if k == 0 else pair_ref.at[base : base + piece, :]
        full_z[pl.ds(here, half), :] = one[0:half, :]
        full_y[pl.ds(here, half), :] = one[half : 2 * half, :]
        full_z[pl.ds(there, half), :] = two[0:half, :]
        full_y[pl.ds(there, half), :] = two[half : 2 * half, :]
        info[k * info_rows : (k + 1) * info_rows, :] = one[2 * half : piece, :]
    terms[...] = jnp.zeros_like(terms)
    chunk = 8
    rank = full_z.shape[1]
    for s in range(slots):
        at = pl.multiple_of(table[slots + s] * edge, edge)
        panel_z = full_z[pl.ds(at, edge), :].astype(f32)
        at = pl.multiple_of(table[2 * slots + s] * edge, edge)
        panel_y = full_y[pl.ds(at, edge), :]
        u = table[s]
        live = u >= 0
        k = lax.rem(jnp.maximum(u, 0) + (ta_count - me), ta_count)
        for f in range(0, frames, chunk):
            part = cube[s, f : f + chunk].reshape(chunk * edge, edge)
            inner = jnp.dot(part, panel_y, preferred_element_type=f32)
            summed = jnp.sum(inner.reshape(chunk, edge, rank) * panel_z[None], axis=1)
            at = pl.ds(pl.multiple_of(k * frames + f, chunk), chunk)
            terms[at, :] += jnp.where(live, summed, 0.0)


def system_kernel(ta_count, slots, edge, info, full_z, full_y, system, inverse, codes):
    rank = full_z.shape[1]
    grid = full_z.shape[0] // edge
    me = lax.axis_index("ta")
    lane = lax.broadcasted_iota(jnp.int32, (1, rank), 1)
    for k in range(ta_count):
        table = info[k * info_rows : (k + 1) * info_rows, :].astype(f32)
        cell = (table[1:2, :] * grid + table[2:3, :]).astype(jnp.int32)
        wanted = table[0:1, :].astype(jnp.int32) == me + 1
        code = jnp.where(wanted, cell, -1)
        for s in range(slots):
            codes[k * slots + s] = jnp.max(jnp.where(lane == s, code, -1))
    eye = lax.broadcasted_iota(jnp.int32, (rank, rank), 0) == lax.broadcasted_iota(
        jnp.int32, (rank, rank), 1
    )
    system[...] = jnp.where(eye, ridge_weight, 0.0).astype(f32)

    @pl.loop(0, ta_count * slots)
    def _(i):
        code = codes[i]

        @pl.when(code >= 0)
        def _():
            at = pl.multiple_of(lax.div(code, grid) * edge, edge)
            panel_z = full_z[pl.ds(at, edge), :]
            at = pl.multiple_of(lax.rem(code, grid) * edge, edge)
            panel_y = full_y[pl.ds(at, edge), :]
            over = (((0,), (0,)), ((), ()))
            gram_z = lax.dot_general(panel_z, panel_z, over, preferred_element_type=f32)
            gram_y = lax.dot_general(panel_y, panel_y, over, preferred_element_type=f32)
            system[...] += gram_z * gram_y

    matrix = system[...]
    down = 1.0 / jnp.sum(jnp.where(eye, matrix, 0.0), axis=1, keepdims=True)
    across = 1.0 / jnp.sum(jnp.where(eye, matrix, 0.0), axis=0, keepdims=True)
    inverse[...] = jnp.where(eye, 2.0 * across, 0.0) - down * matrix * across

    def going(state):
        step, error = state
        return (step < newton_steps) & jnp.logical_not(error <= newton_goal)

    def newton(state):
        guess = inverse[...]
        miss = jnp.where(eye, 1.0, 0.0) - jnp.dot(
            system[...], guess, precision=top, preferred_element_type=f32
        )
        inverse[...] = guess + jnp.dot(guess, miss, precision=top, preferred_element_type=f32)
        return state[0] + 1, jnp.sum(miss * miss)

    _, error = lax.while_loop(going, newton, (jnp.int32(0), jnp.float32(jnp.inf)))

    @pl.when(jnp.logical_not(error <= newton_goal))
    def _():
        inverse[...] = system[...]
        lanes = lax.broadcasted_iota(jnp.int32, (1, rank), 1)
        subs = lax.broadcasted_iota(jnp.int32, (rank, 1), 0)

        @pl.loop(0, rank)
        def _(k):
            whole = inverse[...]
            row = inverse[pl.ds(k, 1), :]
            column = jnp.sum(jnp.where(lanes == k, whole, 0.0), axis=1, keepdims=True)
            pivot = 1.0 / jnp.sum(jnp.where(lanes == k, row, 0.0), axis=1, keepdims=True)
            scaled = jnp.where(lanes == k, 1.0, row) * pivot
            rest = jnp.where(lanes == k, 0.0, whole) - column * scaled
            inverse[...] = jnp.where(subs == k, scaled, rest)


def solve_kernel(ta_count, own, far, system, inverse, rows_out, low_out):
    frames = rows_out.shape[0]
    rhs = own[0:frames, :]
    for k in range(1, ta_count):
        rhs = rhs + far[(k - 1) * frames : k * frames, :]
    dot = functools.partial(jnp.dot, precision=top, preferred_element_type=f32)
    rows = dot(rhs, inverse[...])
    rest = rhs - dot(rows, system[...])
    rows = rows + dot(rest, inverse[...])
    rows_out[...] = rows
    low_out[...] = rows.astype(bf16)


def misfit_kernel(ta_count, edge, table, low, far, full_z, full_y, cube, out, every):
    slots, frames = cube.shape[0], cube.shape[1]
    every[0] = low[...].astype(f32)
    for k in range(1, ta_count):
        every[k] = far[(k - 1) * frames : k * frames, :].astype(f32)
    me = lax.axis_index("ta")
    chunk = 8
    rank = full_z.shape[1]
    lane = lax.broadcasted_iota(jnp.int32, out.shape, 1)
    answer = jnp.zeros(out.shape, f32)
    over = (((1,), (1,)), ((), ()))
    for s in range(slots):
        at = pl.multiple_of(table[slots + s] * edge, edge)
        panel_z = full_z[pl.ds(at, edge), :].astype(f32)
        at = pl.multiple_of(table[2 * slots + s] * edge, edge)
        panel_y = full_y[pl.ds(at, edge), :]
        u = table[s]
        k = lax.rem(me + (ta_count - jnp.maximum(u, 0)), ta_count)
        total = jnp.zeros((8, edge), f32)
        for f in range(0, frames, chunk):
            rows = every[k, f : f + chunk, :]
            outer = (rows[:, None, :] * panel_z[None]).astype(bf16).reshape(chunk * edge, rank)
            model = lax.dot_general(outer, panel_y, over, preferred_element_type=f32)
            off = cube[s, f : f + chunk].reshape(chunk * edge, edge).astype(f32) - model
            total = total + jnp.sum((off * off).reshape(chunk * edge // 8, 8, edge), axis=0)
        mean = jnp.sum(total) * (1.0 / (frames * edge * edge))
        answer = jnp.where((lane == s) & (u >= 0), mean, answer)
    out[...] = answer


def around(x, axis, count):
    if count <= ring_limit:
        turns = [
            lax.ppermute(x, axis, [(i, (i + k) % count) for i in range(count)])
            for k in range(1, count)
        ]
        return jnp.concatenate(turns, axis=0)
    every = lax.all_gather(x, axis, axis=0)
    order = (lax.axis_index(axis) - jnp.arange(1, count)) % count
    return every[order].reshape((count - 1) * x.shape[0], x.shape[1])


def deliver(terms, axis, count):
    frames = terms.shape[0] // count
    if count <= ring_limit:
        turns = [
            lax.ppermute(
                terms[k * frames : (k + 1) * frames],
                axis,
                [(i, (i + k) % count) for i in range(count)],
            )
            for k in range(1, count)
        ]
        return jnp.concatenate(turns, axis=0)
    me = lax.axis_index(axis)
    split = terms.reshape(count, frames, terms.shape[1])
    arrived = lax.all_to_all(
        split[(jnp.arange(count) - me) % count], axis, split_axis=0, concat_axis=0
    )
    order = (me - jnp.arange(1, count)) % count
    return arrived[order].reshape((count - 1) * frames, terms.shape[1])


def body(blocks, qz_factor, qy_factor, block_owner, block_cells):
    ta_count, pb_count = lax.axis_size("ta"), lax.axis_size("pb")
    slots, frames, edge = blocks.shape[2], blocks.shape[3], blocks.shape[4]
    rows, rank = qz_factor.shape
    half = rows // 2
    piece = 2 * half + info_rows
    shape = jax.ShapeDtypeStruct
    packed, rest, table = pl.pallas_call(
        pack_kernel,
        out_shape=[
            shape((piece, rank), bf16),
            shape((2 * half, rank), bf16),
            shape((3 * slots,), jnp.int32),
        ],
        in_specs=[smem_spec] * 2 + [hbm_spec] * 2,
        out_specs=[vmem_spec] * 2 + [smem_spec],
        scratch_shapes=[pltpu.SemaphoreType.DMA((4,))],
        compiler_params=params(4),
        name="pack",
    )(*(held(x) for x in (block_owner, jnp.swapaxes(block_cells, 2, 3), qz_factor, qy_factor)))
    cube = pl.pallas_call(
        load_kernel,
        out_shape=shape((slots, frames, edge, edge), bf16),
        in_specs=[hbm_spec],
        out_specs=vmem_spec,
        scratch_shapes=[pltpu.SemaphoreType.DMA((slots,))],
        compiler_params=params(8),
        cost_estimate=pl.CostEstimate(
            flops=0, transcendentals=0, bytes_accessed=4 * slots * frames * edge * edge
        ),
        name="load",
    )(held(blocks))
    far, cube = lax.optimization_barrier((around(packed, "ta", ta_count), cube))
    pair = lax.ppermute(far, "pb", [(i, i ^ 1) for i in range(pb_count)])
    terms, full_z, full_y, info = pl.pallas_call(
        functools.partial(term_kernel, ta_count, edge),
        out_shape=[
            shape((ta_count * frames, rank), f32),
            shape((ta_count * rows, rank), bf16),
            shape((ta_count * rows, rank), bf16),
            shape((ta_count * info_rows, rank), bf16),
        ],
        in_specs=[smem_spec] + [vmem_spec] * 5,
        out_specs=[vmem_spec] * 4,
        compiler_params=params(16),
        name="terms",
    )(table, packed, rest, far, pair, cube)
    arrived = deliver(terms, "ta", ta_count)
    system, inverse = pl.pallas_call(
        functools.partial(system_kernel, ta_count, slots, edge),
        out_shape=[shape((rank, rank), f32)] * 2,
        in_specs=[vmem_spec] * 3,
        out_specs=[vmem_spec] * 2,
        scratch_shapes=[pltpu.SMEM((ta_count * slots,), jnp.int32)],
        compiler_params=params(16),
        name="system",
    )(info, full_z, full_y)
    new_rows, low = pl.pallas_call(
        functools.partial(solve_kernel, ta_count),
        out_shape=[shape((frames, rank), f32), shape((frames, rank), bf16)],
        in_specs=[vmem_spec] * 4,
        out_specs=[vmem_spec] * 2,
        compiler_params=params(8),
        name="solve",
    )(terms, arrived, system, inverse)
    others = around(low, "ta", ta_count)
    misfit = pl.pallas_call(
        functools.partial(misfit_kernel, ta_count, edge),
        out_shape=shape((1, slots), f32),
        in_specs=[smem_spec] + [vmem_spec] * 5,
        out_specs=vmem_spec,
        scratch_shapes=[pltpu.VMEM((ta_count, frames, rank), f32)],
        compiler_params=params(16),
        name="misfit",
    )(table, low, others, full_z, full_y, cube)
    return (new_rows, misfit.reshape(1, 1, slots))


def solution(mesh):
    placed = (
        P(("series", "ta"), "pb", None, None, None, None),
        P(("series", "ta"), None),
        P(("series", "ta"), None),
        P(("series", "ta"), "pb", None),
        P(("series", "ta"), "pb", None, None),
    )
    return jax.shard_map(
        body,
        mesh=mesh,
        in_specs=placed,
        out_specs=(P(("series", "ta", "pb"), None), P(("series", "ta"), "pb", None)),
        check_vma=False,
    )
```

```python
import functools

import jax
import jax.numpy as jnp
from jax import lax
from jax.experimental import pallas as pl
from jax.experimental.pallas import tpu as pltpu
from jax.sharding import PartitionSpec as P

ridge_weight = 0.1
info_rows = 16
swap_limit = 8
newton_steps = 10
newton_goal = 4e-4
top = lax.Precision.HIGHEST
f32 = jnp.float32
bf16 = jnp.bfloat16

vmem_spec = pl.BlockSpec(memory_space=pltpu.VMEM)
smem_spec = pl.BlockSpec(memory_space=pltpu.SMEM)
hbm_spec = pl.BlockSpec(memory_space=pltpu.HBM)


def held(x):
    return pltpu.with_memory_space_constraint(x, pltpu.HBM)


def params(mib):
    return pltpu.CompilerParams(vmem_limit_bytes=mib * 1024 * 1024)


def pack_kernel(owner_hbm, cells_hbm, z_hbm, y_hbm, half_ref, part_ref, rest_ref, table_ref, owner, cells, sems):
    half = z_hbm.shape[0] // 2
    part = half // 2
    rank = z_hbm.shape[1]
    slots = owner.shape[2]
    column = lax.axis_index("pb")
    core = lax.rem(column, 2)
    side = lax.rem(lax.div(column, 2), 2)
    small = [
        pltpu.make_async_copy(owner_hbm, owner, sems.at[6]),
        pltpu.make_async_copy(cells_hbm, cells, sems.at[7]),
    ]
    copies = []
    pieces = (
        (half_ref, core * half, half),
        (part_ref, core * half + side * part, part),
        (rest_ref, (1 - core) * half, half),
    )
    for i, (target, at, count) in enumerate(pieces):
        for j, source in enumerate((z_hbm, y_hbm)):
            copies.append(
                pltpu.make_async_copy(
                    source.at[pl.ds(pl.multiple_of(at, count), count), :],
                    target.at[j * count : (j + 1) * count, :],
                    sems.at[2 * i + j],
                )
            )
    for copy in small + copies:
        copy.start()
    for copy in small:
        copy.wait()
    shape = (info_rows, rank)
    row = lax.broadcasted_iota(jnp.int32, shape, 0)
    lane = lax.broadcasted_iota(jnp.int32, shape, 1)
    table = jnp.zeros(shape, jnp.int32)
    for s in range(slots):
        values = (owner[0, 0, s], cells[0, 0, 0, s], cells[0, 0, 1, s])
        for r, value in enumerate(values):
            table_ref[r * slots + s] = value
            shown = value + 1 if r == 0 else value
            table = jnp.where((row == r) & (lane == s), shown, table)
    table = table.astype(f32).astype(bf16)
    half_ref[2 * half :, :] = table
    part_ref[2 * part :, :] = table
    for copy in copies:
        copy.wait()


def distance(u, me, swaps):
    u = jnp.maximum(u, 0)
    return lax.bitwise_xor(u, me) if swaps else u


def load_kernel(blocks, cube, sems):
    slots = cube.shape[0]
    copies = [pltpu.make_async_copy(blocks.at[0, 0, s], cube.at[s], sems.at[s]) for s in range(slots)]
    for copy in copies:
        copy.start()
    for copy in copies:
        copy.wait()


def assemble(near, part, rest, first, away, side_away, mate, full_z, full_y, info):
    half = rest.shape[0] // 2
    quarter = half // 2
    rows = 2 * half
    tall = 2 * half + info_rows
    short = 2 * quarter + info_rows
    me = lax.axis_index("ta")
    column = lax.axis_index("pb")
    core = lax.rem(column, 2)
    side = lax.rem(lax.div(column, 2), 2)

    def put(ref, base, at, count):
        at = pl.ds(pl.multiple_of(at, count), count)
        full_z[at, :] = ref[base : base + count, :]
        full_y[at, :] = ref[base + count : base + 2 * count, :]

    info[0:info_rows, :] = near[2 * half :, :]
    put(near, 0, me * rows + core * half, half)
    put(rest, 0, me * rows + (1 - core) * half, half)
    info[info_rows : 2 * info_rows, :] = first[2 * half :, :]
    source = lax.bitwise_xor(me, 1) * rows
    put(first, 0, source + core * half, half)
    put(mate, 0, source + (1 - core) * half, half)
    others = away.shape[0] // short
    for i in range(others):
        source = lax.bitwise_xor(me, i + 2) * rows
        base = i * short
        info[(i + 2) * info_rows : (i + 3) * info_rows, :] = away[base + 2 * quarter : base + short, :]
        for ref, start, which, where in (
            (away, 0, core, side),
            (side_away, 0, core, 1 - side),
            (mate, tall, 1 - core, side),
            (mate, tall + others * short, 1 - core, 1 - side),
        ):
            put(ref, start + base, source + which * half + where * quarter, quarter)


def term_kernel(ta_count, edge, swaps, table, cube, *refs):
    if swaps:
        pieces, (terms, full_z, full_y, info) = refs[:-4], refs[-4:]
        assemble(*pieces, full_z, full_y, info)
    else:
        full_z, full_y, terms = refs
    slots, frames = cube.shape[0], cube.shape[1]
    me = lax.axis_index("ta")
    terms[...] = jnp.zeros_like(terms)
    chunk = 8
    rank = full_z.shape[1]
    for s in range(slots):
        at = pl.multiple_of(table[slots + s] * edge, edge)
        panel_z = full_z[pl.ds(at, edge), :].astype(f32)
        at = pl.multiple_of(table[2 * slots + s] * edge, edge)
        panel_y = full_y[pl.ds(at, edge), :]
        u = table[s]
        live = u >= 0
        k = distance(u, me, swaps)
        for f in range(0, frames, chunk):
            part = cube[s, f : f + chunk].reshape(chunk * edge, edge)
            inner = jnp.dot(part, panel_y, preferred_element_type=f32)
            summed = jnp.sum(inner.reshape(chunk, edge, rank) * panel_z[None], axis=1)
            at = pl.ds(pl.multiple_of(k * frames + f, chunk), chunk)
            terms[at, :] += jnp.where(live, summed, 0.0)


def system_kernel(ta_count, slots, edge, info, full_z, full_y, system, inverse, codes):
    rank = full_z.shape[1]
    grid = full_z.shape[0] // edge
    me = lax.axis_index("ta")
    lane = lax.broadcasted_iota(jnp.int32, (1, rank), 1)
    for k in range(ta_count):
        table = info[k * info_rows : (k + 1) * info_rows, :].astype(f32)
        cell = (table[1:2, :] * grid + table[2:3, :]).astype(jnp.int32)
        wanted = table[0:1, :].astype(jnp.int32) == me + 1
        code = jnp.where(wanted, cell, -1)
        for s in range(slots):
            codes[k * slots + s] = jnp.max(jnp.where(lane == s, code, -1))
    eye = lax.broadcasted_iota(jnp.int32, (rank, rank), 0) == lax.broadcasted_iota(
        jnp.int32, (rank, rank), 1
    )
    system[...] = jnp.where(eye, ridge_weight, 0.0).astype(f32)

    @pl.loop(0, ta_count * slots)
    def _(i):
        code = codes[i]

        @pl.when(code >= 0)
        def _():
            at = pl.multiple_of(lax.div(code, grid) * edge, edge)
            panel_z = full_z[pl.ds(at, edge), :]
            at = pl.multiple_of(lax.rem(code, grid) * edge, edge)
            panel_y = full_y[pl.ds(at, edge), :]
            over = (((0,), (0,)), ((), ()))
            gram_z = lax.dot_general(panel_z, panel_z, over, preferred_element_type=f32)
            gram_y = lax.dot_general(panel_y, panel_y, over, preferred_element_type=f32)
            system[...] += gram_z * gram_y

    matrix = system[...]
    down = 1.0 / jnp.sum(jnp.where(eye, matrix, 0.0), axis=1, keepdims=True)
    across = 1.0 / jnp.sum(jnp.where(eye, matrix, 0.0), axis=0, keepdims=True)
    inverse[...] = jnp.where(eye, 2.0 * across, 0.0) - down * matrix * across

    def going(state):
        step, error = state
        return (step < newton_steps) & jnp.logical_not(error <= newton_goal)

    def newton(state):
        guess = inverse[...]
        miss = jnp.where(eye, 1.0, 0.0) - jnp.dot(
            system[...], guess, precision=top, preferred_element_type=f32
        )
        inverse[...] = guess + jnp.dot(guess, miss, precision=top, preferred_element_type=f32)
        return state[0] + 1, jnp.sum(miss * miss)

    _, error = lax.while_loop(going, newton, (jnp.int32(0), jnp.float32(jnp.inf)))

    @pl.when(jnp.logical_not(error <= newton_goal))
    def _():
        inverse[...] = system[...]
        lanes = lax.broadcasted_iota(jnp.int32, (1, rank), 1)
        subs = lax.broadcasted_iota(jnp.int32, (rank, 1), 0)

        @pl.loop(0, rank)
        def _(k):
            whole = inverse[...]
            row = inverse[pl.ds(k, 1), :]
            column = jnp.sum(jnp.where(lanes == k, whole, 0.0), axis=1, keepdims=True)
            pivot = 1.0 / jnp.sum(jnp.where(lanes == k, row, 0.0), axis=1, keepdims=True)
            scaled = jnp.where(lanes == k, 1.0, row) * pivot
            rest = jnp.where(lanes == k, 0.0, whole) - column * scaled
            inverse[...] = jnp.where(subs == k, scaled, rest)


def solve_kernel(ta_count, swaps, own, far, system, inverse, rows_out, low_out):
    frames = rows_out.shape[0]
    if swaps:
        rhs = own[0:frames, :]
        for k in range(1, ta_count):
            rhs = rhs + far[(k - 1) * frames : k * frames, :]
    else:
        rhs = far[0:frames, :]
        for k in range(1, ta_count):
            rhs = rhs + far[k * frames : (k + 1) * frames, :]
    dot = functools.partial(jnp.dot, precision=top, preferred_element_type=f32)
    rows = dot(rhs, inverse[...])
    rest = rhs - dot(rows, system[...])
    rows = rows + dot(rest, inverse[...])
    rows_out[...] = rows
    low_out[...] = rows.astype(bf16)


def misfit_kernel(ta_count, edge, swaps, table, low, far, full_z, full_y, cube, out, every):
    slots, frames = cube.shape[0], cube.shape[1]
    if swaps:
        every[0] = low[...].astype(f32)
    first = 1 if swaps else 0
    for k in range(first, ta_count):
        every[k] = far[(k - first) * frames : (k + 1 - first) * frames, :].astype(f32)
    me = lax.axis_index("ta")
    chunk = 8
    rank = full_z.shape[1]
    lane = lax.broadcasted_iota(jnp.int32, out.shape, 1)
    answer = jnp.zeros(out.shape, f32)
    over = (((1,), (1,)), ((), ()))
    for s in range(slots):
        at = pl.multiple_of(table[slots + s] * edge, edge)
        panel_z = full_z[pl.ds(at, edge), :].astype(f32)
        at = pl.multiple_of(table[2 * slots + s] * edge, edge)
        panel_y = full_y[pl.ds(at, edge), :]
        u = table[s]
        k = distance(u, me, swaps)
        total = jnp.zeros((8, edge), f32)
        for f in range(0, frames, chunk):
            rows = every[k, f : f + chunk, :]
            outer = (rows[:, None, :] * panel_z[None]).astype(bf16).reshape(chunk * edge, rank)
            model = lax.dot_general(outer, panel_y, over, preferred_element_type=f32)
            off = cube[s, f : f + chunk].reshape(chunk * edge, edge).astype(f32) - model
            total = total + jnp.sum((off * off).reshape(chunk * edge // 8, 8, edge), axis=0)
        mean = jnp.sum(total) * (1.0 / (frames * edge * edge))
        answer = jnp.where((lane == s) & (u >= 0), mean, answer)
    out[...] = answer


def swap(x, axis, count, k):
    return lax.ppermute(x, axis, [(i, i ^ k) for i in range(count)])


def body(blocks, qz_factor, qy_factor, block_owner, block_cells):
    ta_count, pb_count = lax.axis_size("ta"), lax.axis_size("pb")
    slots, frames, edge = blocks.shape[2], blocks.shape[3], blocks.shape[4]
    rows, rank = qz_factor.shape
    half, quarter = rows // 2, rows // 4
    swaps = (
        ta_count in (4, swap_limit) and pb_count % 4 == 0 and rows % 64 == 0
    )
    shape = jax.ShapeDtypeStruct
    cells = jnp.swapaxes(block_cells, 2, 3)
    full = [shape((ta_count * rows, rank), bf16)] * 2
    cube = pl.pallas_call(
        load_kernel,
        out_shape=shape((slots, frames, edge, edge), bf16),
        in_specs=[hbm_spec],
        out_specs=vmem_spec,
        scratch_shapes=[pltpu.SemaphoreType.DMA((slots,))],
        compiler_params=params(8),
        cost_estimate=pl.CostEstimate(
            flops=0, transcendentals=0, bytes_accessed=4 * slots * frames * edge * edge
        ),
        name="load",
    )(held(blocks))
    if swaps:
        near, part, rest, table = pl.pallas_call(
            pack_kernel,
            out_shape=[
                shape((2 * half + info_rows, rank), bf16),
                shape((2 * quarter + info_rows, rank), bf16),
                shape((2 * half, rank), bf16),
                shape((3 * slots,), jnp.int32),
            ],
            in_specs=[hbm_spec] * 4,
            out_specs=[vmem_spec] * 3 + [smem_spec],
            scratch_shapes=[
                pltpu.SMEM(block_owner.shape, jnp.int32),
                pltpu.SMEM(cells.shape, jnp.int32),
                pltpu.SemaphoreType.DMA((8,)),
            ],
            compiler_params=params(4),
            name="pack",
        )(*(held(x) for x in (block_owner, cells, qz_factor, qy_factor)))
        first = swap(near, "ta", ta_count, 1)
        away = jnp.concatenate([swap(part, "ta", ta_count, k) for k in range(2, ta_count)], axis=0)
        away, cube = lax.optimization_barrier((away, cube))
        side_away = swap(away, "pb", pb_count, 2)
        mate = swap(jnp.concatenate([first, away, side_away], axis=0), "pb", pb_count, 1)
        pieces = (near, part, rest, first, away, side_away, mate)
        made = full + [shape((ta_count * info_rows, rank), bf16)]
    else:
        table = jnp.concatenate([block_owner.reshape(slots), cells.reshape(2 * slots)])
        pieces = (
            lax.all_gather(qz_factor, "ta", axis=0, tiled=True),
            lax.all_gather(qy_factor, "ta", axis=0, tiled=True),
        )
        made = []
        shown = jnp.zeros((info_rows, rank), jnp.int32)
        shown = shown.at[0, :slots].set(table[:slots] + 1)
        shown = shown.at[1:3, :slots].set(table[slots:].reshape(2, slots))
        info = lax.all_gather(shown.astype(bf16), "ta", axis=0, tiled=True)
    out = pl.pallas_call(
        functools.partial(term_kernel, ta_count, edge, swaps),
        out_shape=[shape((ta_count * frames, rank), f32)] + made,
        in_specs=[smem_spec] + [vmem_spec] * (1 + len(pieces)),
        out_specs=[vmem_spec] * (1 + len(made)),
        compiler_params=params(16),
        name="terms",
    )(table, cube, *pieces)
    terms = out[0]
    if swaps:
        full_z, full_y, info = out[1:]
        arrived = jnp.concatenate(
            [
                swap(terms[k * frames : (k + 1) * frames], "ta", ta_count, k)
                for k in range(1, ta_count)
            ],
            axis=0,
        )
    else:
        full_z, full_y = pieces
        arrived = lax.all_to_all(terms, "ta", split_axis=0, concat_axis=0, tiled=True)
    system, inverse = pl.pallas_call(
        functools.partial(system_kernel, ta_count, slots, edge),
        out_shape=[shape((rank, rank), f32)] * 2,
        in_specs=[vmem_spec] * 3,
        out_specs=[vmem_spec] * 2,
        scratch_shapes=[pltpu.SMEM((ta_count * slots,), jnp.int32)],
        compiler_params=params(16),
        name="system",
    )(info, full_z, full_y)
    new_rows, low = pl.pallas_call(
        functools.partial(solve_kernel, ta_count, swaps),
        out_shape=[shape((frames, rank), f32), shape((frames, rank), bf16)],
        in_specs=[vmem_spec] * 4,
        out_specs=[vmem_spec] * 2,
        compiler_params=params(8),
        name="solve",
    )(terms, arrived, system, inverse)
    if swaps:
        others = jnp.concatenate([swap(low, "ta", ta_count, k) for k in range(1, ta_count)], axis=0)
    else:
        others = lax.all_gather(low, "ta", axis=0, tiled=True)
    misfit = pl.pallas_call(
        functools.partial(misfit_kernel, ta_count, edge, swaps),
        out_shape=shape((1, slots), f32),
        in_specs=[smem_spec] + [vmem_spec] * 5,
        out_specs=vmem_spec,
        scratch_shapes=[pltpu.VMEM((ta_count, frames, rank), f32)],
        compiler_params=params(16),
        name="misfit",
    )(table, low, others, full_z, full_y, cube)
    return (new_rows, misfit.reshape(1, 1, slots))


def solution(mesh):
    placed = (
        P(("series", "ta"), "pb", None, None, None, None),
        P(("series", "ta"), None),
        P(("series", "ta"), None),
        P(("series", "ta"), "pb", None),
        P(("series", "ta"), "pb", None, None),
    )
    return jax.shard_map(
        body,
        mesh=mesh,
        in_specs=placed,
        out_specs=(P(("series", "ta", "pb"), None), P(("series", "ta"), "pb", None)),
        check_vma=False,
    )
```

```python
import functools

import jax
import jax.numpy as jnp
from jax import lax
from jax.experimental import pallas as pl
from jax.experimental.pallas import tpu as pltpu
from jax.sharding import PartitionSpec as P

ridge_weight = 0.1
info_rows = 16
swap_limit = 8
newton_steps = 10
newton_goal = 4e-4
top = lax.Precision.HIGHEST
f32 = jnp.float32
bf16 = jnp.bfloat16

vmem_spec = pl.BlockSpec(memory_space=pltpu.VMEM)
smem_spec = pl.BlockSpec(memory_space=pltpu.SMEM)
hbm_spec = pl.BlockSpec(memory_space=pltpu.HBM)


def held(x):
    return pltpu.with_memory_space_constraint(x, pltpu.HBM)


def params(mib):
    return pltpu.CompilerParams(vmem_limit_bytes=mib * 1024 * 1024)


def pack_kernel(owner_hbm, cells_hbm, z_hbm, y_hbm, half_ref, part_ref, rest_ref, table_ref, owner, cells, sems):
    half = z_hbm.shape[0] // 2
    part = half // 2
    rank = z_hbm.shape[1]
    slots = owner.shape[2]
    column = lax.axis_index("pb")
    core = lax.rem(column, 2)
    side = lax.rem(lax.div(column, 2), 2)
    small = [
        pltpu.make_async_copy(owner_hbm, owner, sems.at[6]),
        pltpu.make_async_copy(cells_hbm, cells, sems.at[7]),
    ]
    copies = []
    pieces = (
        (half_ref, core * half, half),
        (part_ref, core * half + side * part, part),
        (rest_ref, (1 - core) * half, half),
    )
    for i, (target, at, count) in enumerate(pieces):
        for j, source in enumerate((z_hbm, y_hbm)):
            copies.append(
                pltpu.make_async_copy(
                    source.at[pl.ds(pl.multiple_of(at, count), count), :],
                    target.at[j * count : (j + 1) * count, :],
                    sems.at[2 * i + j],
                )
            )
    for copy in small + copies:
        copy.start()
    for copy in small:
        copy.wait()
    shape = (info_rows, rank)
    row = lax.broadcasted_iota(jnp.int32, shape, 0)
    lane = lax.broadcasted_iota(jnp.int32, shape, 1)
    table = jnp.zeros(shape, jnp.int32)
    for s in range(slots):
        values = (owner[0, 0, s], cells[0, 0, 0, s], cells[0, 0, 1, s])
        for r, value in enumerate(values):
            table_ref[r * slots + s] = value
            shown = value + 1 if r == 0 else value
            table = jnp.where((row == r) & (lane == s), shown, table)
    table = table.astype(f32).astype(bf16)
    half_ref[2 * half :, :] = table
    part_ref[2 * part :, :] = table
    for copy in copies:
        copy.wait()


def distance(u, me, swaps):
    u = jnp.maximum(u, 0)
    return lax.bitwise_xor(u, me) if swaps else u


def load_kernel(blocks, cube, sems):
    slots = cube.shape[0]
    copies = [pltpu.make_async_copy(blocks.at[0, 0, s], cube.at[s], sems.at[s]) for s in range(slots)]
    for copy in copies:
        copy.start()
    for copy in copies:
        copy.wait()


def assemble(near, part, rest, first, away, side_away, mate, full_z, full_y, info):
    half = rest.shape[0] // 2
    quarter = half // 2
    rows = 2 * half
    tall = 2 * half + info_rows
    short = 2 * quarter + info_rows
    me = lax.axis_index("ta")
    column = lax.axis_index("pb")
    core = lax.rem(column, 2)
    side = lax.rem(lax.div(column, 2), 2)

    def put(ref, base, at, count):
        at = pl.ds(pl.multiple_of(at, count), count)
        full_z[at, :] = ref[base : base + count, :]
        full_y[at, :] = ref[base + count : base + 2 * count, :]

    info[0:info_rows, :] = near[2 * half :, :]
    put(near, 0, me * rows + core * half, half)
    put(rest, 0, me * rows + (1 - core) * half, half)
    info[info_rows : 2 * info_rows, :] = first[2 * half :, :]
    source = lax.bitwise_xor(me, 1) * rows
    put(first, 0, source + core * half, half)
    put(mate, 0, source + (1 - core) * half, half)
    others = away.shape[0] // short
    for i in range(others):
        source = lax.bitwise_xor(me, i + 2) * rows
        base = i * short
        info[(i + 2) * info_rows : (i + 3) * info_rows, :] = away[base + 2 * quarter : base + short, :]
        for ref, start, which, where in (
            (away, 0, core, side),
            (side_away, 0, core, 1 - side),
            (mate, tall, 1 - core, side),
            (mate, tall + others * short, 1 - core, 1 - side),
        ):
            put(ref, start + base, source + which * half + where * quarter, quarter)


def term_kernel(ta_count, edge, swaps, table, cube, *refs):
    if swaps:
        pieces, (terms, full_z, full_y, info) = refs[:-4], refs[-4:]
        assemble(*pieces, full_z, full_y, info)
    else:
        full_z, full_y, terms = refs
    slots, frames = cube.shape[0], cube.shape[1]
    me = lax.axis_index("ta")
    terms[...] = jnp.zeros_like(terms)
    chunk = 8
    rank = full_z.shape[1]
    for s in range(slots):
        at = pl.multiple_of(table[slots + s] * edge, edge)
        panel_z = full_z[pl.ds(at, edge), :].astype(f32)
        at = pl.multiple_of(table[2 * slots + s] * edge, edge)
        panel_y = full_y[pl.ds(at, edge), :]
        u = table[s]
        live = u >= 0
        k = distance(u, me, swaps)
        for f in range(0, frames, chunk):
            part = cube[s, f : f + chunk].reshape(chunk * edge, edge)
            inner = jnp.dot(part, panel_y, preferred_element_type=f32)
            summed = jnp.sum(inner.reshape(chunk, edge, rank) * panel_z[None], axis=1)
            at = pl.ds(pl.multiple_of(k * frames + f, chunk), chunk)
            terms[at, :] += jnp.where(live, summed, 0.0)


def system_kernel(ta_count, slots, edge, info, full_z, full_y, system, inverse, codes):
    rank = full_z.shape[1]
    grid = full_z.shape[0] // edge
    me = lax.axis_index("ta")
    lane = lax.broadcasted_iota(jnp.int32, (1, rank), 1)
    for k in range(ta_count):
        table = info[k * info_rows : (k + 1) * info_rows, :].astype(f32)
        cell = (table[1:2, :] * grid + table[2:3, :]).astype(jnp.int32)
        wanted = table[0:1, :].astype(jnp.int32) == me + 1
        code = jnp.where(wanted, cell, -1)
        for s in range(slots):
            codes[k * slots + s] = jnp.max(jnp.where(lane == s, code, -1))
    eye = lax.broadcasted_iota(jnp.int32, (rank, rank), 0) == lax.broadcasted_iota(
        jnp.int32, (rank, rank), 1
    )
    system[...] = jnp.where(eye, ridge_weight, 0.0).astype(f32)

    @pl.loop(0, ta_count * slots)
    def _(i):
        code = codes[i]

        @pl.when(code >= 0)
        def _():
            at = pl.multiple_of(lax.div(code, grid) * edge, edge)
            panel_z = full_z[pl.ds(at, edge), :]
            at = pl.multiple_of(lax.rem(code, grid) * edge, edge)
            panel_y = full_y[pl.ds(at, edge), :]
            over = (((0,), (0,)), ((), ()))
            gram_z = lax.dot_general(panel_z, panel_z, over, preferred_element_type=f32)
            gram_y = lax.dot_general(panel_y, panel_y, over, preferred_element_type=f32)
            system[...] += gram_z * gram_y

    matrix = system[...]
    down = 1.0 / jnp.sum(jnp.where(eye, matrix, 0.0), axis=1, keepdims=True)
    across = 1.0 / jnp.sum(jnp.where(eye, matrix, 0.0), axis=0, keepdims=True)
    inverse[...] = jnp.where(eye, 2.0 * across, 0.0) - down * matrix * across

    def going(state):
        step, error = state
        return (step < newton_steps) & jnp.logical_not(error <= newton_goal)

    def newton(state):
        guess = inverse[...]
        miss = jnp.where(eye, 1.0, 0.0) - jnp.dot(
            system[...], guess, precision=top, preferred_element_type=f32
        )
        inverse[...] = guess + jnp.dot(guess, miss, precision=top, preferred_element_type=f32)
        return state[0] + 1, jnp.sum(miss * miss)

    _, error = lax.while_loop(going, newton, (jnp.int32(0), jnp.float32(jnp.inf)))

    @pl.when(jnp.logical_not(error <= newton_goal))
    def _():
        inverse[...] = system[...]
        lanes = lax.broadcasted_iota(jnp.int32, (1, rank), 1)
        subs = lax.broadcasted_iota(jnp.int32, (rank, 1), 0)

        @pl.loop(0, rank)
        def _(k):
            whole = inverse[...]
            row = inverse[pl.ds(k, 1), :]
            column = jnp.sum(jnp.where(lanes == k, whole, 0.0), axis=1, keepdims=True)
            pivot = 1.0 / jnp.sum(jnp.where(lanes == k, row, 0.0), axis=1, keepdims=True)
            scaled = jnp.where(lanes == k, 1.0, row) * pivot
            rest = jnp.where(lanes == k, 0.0, whole) - column * scaled
            inverse[...] = jnp.where(subs == k, scaled, rest)


def solve_kernel(ta_count, swaps, own, far, system, inverse, rows_out, low_out):
    frames = rows_out.shape[0]
    if swaps:
        rhs = own[0:frames, :]
        for k in range(1, ta_count):
            rhs = rhs + far[(k - 1) * frames : k * frames, :]
    else:
        rhs = far[0:frames, :]
        for k in range(1, ta_count):
            rhs = rhs + far[k * frames : (k + 1) * frames, :]
    dot = functools.partial(jnp.dot, precision=top, preferred_element_type=f32)
    rows = dot(rhs, inverse[...])
    rest = rhs - dot(rows, system[...])
    rows = rows + dot(rest, inverse[...])
    rows_out[...] = rows
    low_out[...] = rows.astype(bf16)


def misfit_kernel(ta_count, edge, swaps, table, low, far, full_z, full_y, cube, out, every):
    slots, frames = cube.shape[0], cube.shape[1]
    if swaps:
        every[0] = low[...].astype(f32)
    first = 1 if swaps else 0
    for k in range(first, ta_count):
        every[k] = far[(k - first) * frames : (k + 1 - first) * frames, :].astype(f32)
    me = lax.axis_index("ta")
    chunk = 8
    rank = full_z.shape[1]
    lane = lax.broadcasted_iota(jnp.int32, out.shape, 1)
    answer = jnp.zeros(out.shape, f32)
    over = (((1,), (1,)), ((), ()))
    for s in range(slots):
        at = pl.multiple_of(table[slots + s] * edge, edge)
        panel_z = full_z[pl.ds(at, edge), :].astype(f32)
        at = pl.multiple_of(table[2 * slots + s] * edge, edge)
        panel_y = full_y[pl.ds(at, edge), :]
        u = table[s]
        k = distance(u, me, swaps)
        total = jnp.zeros((8, edge), f32)
        for f in range(0, frames, chunk):
            rows = every[k, f : f + chunk, :]
            outer = (rows[:, None, :] * panel_z[None]).astype(bf16).reshape(chunk * edge, rank)
            model = lax.dot_general(outer, panel_y, over, preferred_element_type=f32)
            off = cube[s, f : f + chunk].reshape(chunk * edge, edge).astype(f32) - model
            total = total + jnp.sum((off * off).reshape(chunk * edge // 8, 8, edge), axis=0)
        mean = jnp.sum(total) * (1.0 / (frames * edge * edge))
        answer = jnp.where((lane == s) & (u >= 0), mean, answer)
    out[...] = answer


def swap(x, axis, count, k):
    return lax.ppermute(x, axis, [(i, i ^ k) for i in range(count)])


def body(blocks, qz_factor, qy_factor, block_owner, block_cells):
    ta_count, pb_count = lax.axis_size("ta"), lax.axis_size("pb")
    slots, frames, edge = blocks.shape[2], blocks.shape[3], blocks.shape[4]
    rows, rank = qz_factor.shape
    half, quarter = rows // 2, rows // 4
    swaps = (
        ta_count in (4, swap_limit) and pb_count % 4 == 0 and rows % 64 == 0
    )
    shape = jax.ShapeDtypeStruct
    cells = jnp.swapaxes(block_cells, 2, 3)
    full = [shape((ta_count * rows, rank), bf16)] * 2
    load = pl.pallas_call(
        load_kernel,
        out_shape=shape((slots, frames, edge, edge), bf16),
        in_specs=[hbm_spec],
        out_specs=vmem_spec,
        scratch_shapes=[pltpu.SemaphoreType.DMA((slots,))],
        compiler_params=params(8),
        cost_estimate=pl.CostEstimate(
            flops=0, transcendentals=0, bytes_accessed=4 * slots * frames * edge * edge
        ),
        name="load",
    )
    if swaps:
        near, part, rest, table = pl.pallas_call(
            pack_kernel,
            out_shape=[
                shape((2 * half + info_rows, rank), bf16),
                shape((2 * quarter + info_rows, rank), bf16),
                shape((2 * half, rank), bf16),
                shape((3 * slots,), jnp.int32),
            ],
            in_specs=[hbm_spec] * 4,
            out_specs=[vmem_spec] * 3 + [smem_spec],
            scratch_shapes=[
                pltpu.SMEM(block_owner.shape, jnp.int32),
                pltpu.SMEM(cells.shape, jnp.int32),
                pltpu.SemaphoreType.DMA((8,)),
            ],
            compiler_params=params(4),
            name="pack",
        )(*(held(x) for x in (block_owner, cells, qz_factor, qy_factor)))
        first = swap(near, "ta", ta_count, 1)
        away = jnp.concatenate([swap(part, "ta", ta_count, k) for k in range(2, ta_count)], axis=0)
        first, away, blocks = lax.optimization_barrier((first, away, blocks))
        side_away, cube = lax.optimization_barrier(
            (swap(away, "pb", pb_count, 2), load(held(blocks)))
        )
        mate = swap(jnp.concatenate([first, away, side_away], axis=0), "pb", pb_count, 1)
        pieces = (near, part, rest, first, away, side_away, mate)
        made = full + [shape((ta_count * info_rows, rank), bf16)]
    else:
        cube = load(held(blocks))
        table = jnp.concatenate([block_owner.reshape(slots), cells.reshape(2 * slots)])
        pieces = (
            lax.all_gather(qz_factor, "ta", axis=0, tiled=True),
            lax.all_gather(qy_factor, "ta", axis=0, tiled=True),
        )
        made = []
        shown = jnp.zeros((info_rows, rank), jnp.int32)
        shown = shown.at[0, :slots].set(table[:slots] + 1)
        shown = shown.at[1:3, :slots].set(table[slots:].reshape(2, slots))
        info = lax.all_gather(shown.astype(bf16), "ta", axis=0, tiled=True)
    out = pl.pallas_call(
        functools.partial(term_kernel, ta_count, edge, swaps),
        out_shape=[shape((ta_count * frames, rank), f32)] + made,
        in_specs=[smem_spec] + [vmem_spec] * (1 + len(pieces)),
        out_specs=[vmem_spec] * (1 + len(made)),
        compiler_params=params(16),
        name="terms",
    )(table, cube, *pieces)
    terms = out[0]
    if swaps:
        full_z, full_y, info = out[1:]
        arrived = jnp.concatenate(
            [
                swap(terms[k * frames : (k + 1) * frames], "ta", ta_count, k)
                for k in range(1, ta_count)
            ],
            axis=0,
        )
    else:
        full_z, full_y = pieces
        arrived = lax.all_to_all(terms, "ta", split_axis=0, concat_axis=0, tiled=True)
    system, inverse = pl.pallas_call(
        functools.partial(system_kernel, ta_count, slots, edge),
        out_shape=[shape((rank, rank), f32)] * 2,
        in_specs=[vmem_spec] * 3,
        out_specs=[vmem_spec] * 2,
        scratch_shapes=[pltpu.SMEM((ta_count * slots,), jnp.int32)],
        compiler_params=params(16),
        name="system",
    )(info, full_z, full_y)
    new_rows, low = pl.pallas_call(
        functools.partial(solve_kernel, ta_count, swaps),
        out_shape=[shape((frames, rank), f32), shape((frames, rank), bf16)],
        in_specs=[vmem_spec] * 4,
        out_specs=[vmem_spec] * 2,
        compiler_params=params(8),
        name="solve",
    )(terms, arrived, system, inverse)
    if swaps:
        others = jnp.concatenate([swap(low, "ta", ta_count, k) for k in range(1, ta_count)], axis=0)
    else:
        others = lax.all_gather(low, "ta", axis=0, tiled=True)
    misfit = pl.pallas_call(
        functools.partial(misfit_kernel, ta_count, edge, swaps),
        out_shape=shape((1, slots), f32),
        in_specs=[smem_spec] + [vmem_spec] * 5,
        out_specs=vmem_spec,
        scratch_shapes=[pltpu.VMEM((ta_count, frames, rank), f32)],
        compiler_params=params(16),
        name="misfit",
    )(table, low, others, full_z, full_y, cube)
    return (new_rows, misfit.reshape(1, 1, slots))


def solution(mesh):
    placed = (
        P(("series", "ta"), "pb", None, None, None, None),
        P(("series", "ta"), None),
        P(("series", "ta"), None),
        P(("series", "ta"), "pb", None),
        P(("series", "ta"), "pb", None, None),
    )
    return jax.shard_map(
        body,
        mesh=mesh,
        in_specs=placed,
        out_specs=(P(("series", "ta", "pb"), None), P(("series", "ta"), "pb", None)),
        check_vma=False,
    )
```

```python
import functools

import jax
import jax.numpy as jnp
from jax import lax
from jax.experimental import pallas as pl
from jax.experimental.pallas import tpu as pltpu
from jax.sharding import PartitionSpec as P

ridge_weight = 0.1
info_rows = 16
swap_limit = 8
newton_steps = 10
newton_goal = 0.25
solve_goal = 2e-6
top = lax.Precision.HIGHEST
f32 = jnp.float32
bf16 = jnp.bfloat16

vmem_spec = pl.BlockSpec(memory_space=pltpu.VMEM)
smem_spec = pl.BlockSpec(memory_space=pltpu.SMEM)
hbm_spec = pl.BlockSpec(memory_space=pltpu.HBM)


def held(x):
    return pltpu.with_memory_space_constraint(x, pltpu.HBM)


def params(mib):
    return pltpu.CompilerParams(vmem_limit_bytes=mib * 1024 * 1024)


def pack_kernel(owner_hbm, cells_hbm, z_hbm, y_hbm, half_ref, part_ref, rest_ref, table_ref, owner, cells, sems):
    half = z_hbm.shape[0] // 2
    part = half // 2
    rank = z_hbm.shape[1]
    slots = owner.shape[2]
    column = lax.axis_index("pb")
    core = lax.rem(column, 2)
    side = lax.rem(lax.div(column, 2), 2)
    small = [
        pltpu.make_async_copy(owner_hbm, owner, sems.at[6]),
        pltpu.make_async_copy(cells_hbm, cells, sems.at[7]),
    ]
    copies = []
    pieces = (
        (half_ref, core * half, half),
        (part_ref, core * half + side * part, part),
        (rest_ref, (1 - core) * half, half),
    )
    for i, (target, at, count) in enumerate(pieces):
        for j, source in enumerate((z_hbm, y_hbm)):
            copies.append(
                pltpu.make_async_copy(
                    source.at[pl.ds(pl.multiple_of(at, count), count), :],
                    target.at[j * count : (j + 1) * count, :],
                    sems.at[2 * i + j],
                )
            )
    for copy in small + copies:
        copy.start()
    for copy in small:
        copy.wait()
    shape = (info_rows, rank)
    row = lax.broadcasted_iota(jnp.int32, shape, 0)
    lane = lax.broadcasted_iota(jnp.int32, shape, 1)
    table = jnp.zeros(shape, jnp.int32)
    for s in range(slots):
        values = (owner[0, 0, s], cells[0, 0, 0, s], cells[0, 0, 1, s])
        for r, value in enumerate(values):
            table_ref[r * slots + s] = value
            shown = value + 1 if r == 0 else value
            table = jnp.where((row == r) & (lane == s), shown, table)
    table = table.astype(f32).astype(bf16)
    half_ref[2 * half :, :] = table
    part_ref[2 * part :, :] = table
    for copy in copies:
        copy.wait()


def distance(u, me, swaps):
    u = jnp.maximum(u, 0)
    return lax.bitwise_xor(u, me) if swaps else u


def load_kernel(tables, blocks, *refs):
    infos, (cube, found, sems) = refs[:-3], refs[-3:]
    slots = cube.shape[0]
    copies = [pltpu.make_async_copy(blocks.at[0, 0, s], cube.at[s], sems.at[s]) for s in range(slots)]
    for copy in copies:
        copy.start()
    rank = infos[0].shape[1]
    me = lax.axis_index("ta")
    grid = tables[0]
    lane = lax.broadcasted_iota(jnp.int32, (1, rank), 1)
    codes = []
    for which, base in tables[1:]:
        table = infos[which][base : base + info_rows, :].astype(f32)
        cell = (table[1:2, :] * grid + table[2:3, :]).astype(jnp.int32)
        wanted = table[0:1, :].astype(jnp.int32) == me + 1
        code = jnp.where(wanted, cell, -1)
        codes += [jnp.max(jnp.where(lane == s, code, -1)) for s in range(slots)]
    count = jnp.int32(0)
    for code in codes:
        found[1 + count] = code
        count = count + (code >= 0).astype(jnp.int32)
    found[0] = count
    for copy in copies:
        copy.wait()


def assemble(near, rest, first, away, side_away, mate, side_mate, full_z, full_y):
    half = rest.shape[0] // 2
    quarter = half // 2
    rows = 2 * half
    tall = 2 * half + info_rows
    short = 2 * quarter + info_rows
    me = lax.axis_index("ta")
    column = lax.axis_index("pb")
    core = lax.rem(column, 2)
    side = lax.rem(lax.div(column, 2), 2)

    def put(ref, base, at, count):
        at = pl.ds(pl.multiple_of(at, count), count)
        full_z[at, :] = ref[base : base + count, :]
        full_y[at, :] = ref[base + count : base + 2 * count, :]

    put(near, 0, me * rows + core * half, half)
    put(rest, 0, me * rows + (1 - core) * half, half)
    source = lax.bitwise_xor(me, 1) * rows
    put(first, 0, source + core * half, half)
    put(mate, 0, source + (1 - core) * half, half)
    others = away.shape[0] // short
    for i in range(others):
        source = lax.bitwise_xor(me, i + 2) * rows
        base = i * short
        for ref, start, which, where in (
            (away, 0, core, side),
            (side_away, 0, core, 1 - side),
            (mate, tall, 1 - core, side),
            (side_mate, 0, 1 - core, 1 - side),
        ):
            put(ref, start + base, source + which * half + where * quarter, quarter)


def term_kernel(ta_count, edge, swaps, table, cube, *refs):
    if swaps:
        pieces, (terms, full_z, full_y) = refs[:-3], refs[-3:]
        assemble(*pieces, full_z, full_y)
    else:
        full_z, full_y, terms = refs
    slots, frames = cube.shape[0], cube.shape[1]
    me = lax.axis_index("ta")
    terms[...] = jnp.zeros_like(terms)
    chunk = 8
    rank = full_z.shape[1]
    for s in range(slots):
        at = pl.multiple_of(table[slots + s] * edge, edge)
        panel_z = full_z[pl.ds(at, edge), :].astype(f32)
        at = pl.multiple_of(table[2 * slots + s] * edge, edge)
        panel_y = full_y[pl.ds(at, edge), :]
        u = table[s]
        live = u >= 0
        k = distance(u, me, swaps)
        for f in range(0, frames, chunk):
            part = cube[s, f : f + chunk].reshape(chunk * edge, edge)
            inner = jnp.dot(part, panel_y, preferred_element_type=f32)
            summed = jnp.sum(inner.reshape(chunk, edge, rank) * panel_z[None], axis=1)
            at = pl.ds(pl.multiple_of(k * frames + f, chunk), chunk)
            terms[at, :] += jnp.where(live, summed, 0.0)


def system_kernel(edge, found, full_z, full_y, system, high, mid, low, inverse, guess_ref):
    rank = full_z.shape[1]
    grid = full_z.shape[0] // edge
    count = found[0]
    eye = lax.broadcasted_iota(jnp.int32, (rank, rank), 0) == lax.broadcasted_iota(
        jnp.int32, (rank, rank), 1
    )
    system[...] = jnp.where(eye, ridge_weight, 0.0).astype(f32)

    def product(code):
        over = (((0,), (0,)), ((), ()))
        at = pl.multiple_of(lax.div(code, grid) * edge, edge)
        panel_z = full_z[pl.ds(at, edge), :]
        at = pl.multiple_of(lax.rem(code, grid) * edge, edge)
        panel_y = full_y[pl.ds(at, edge), :]
        gram_z = lax.dot_general(panel_z, panel_z, over, preferred_element_type=f32)
        gram_y = lax.dot_general(panel_y, panel_y, over, preferred_element_type=f32)
        return gram_z * gram_y

    @pl.loop(0, lax.div(count + 1, 2))
    def _(j):
        one = found[1 + 2 * j]
        paired = 2 * j + 1 < count
        two = jnp.where(paired, found[2 + 2 * j], one)
        system[...] += product(one) + product(two) * jnp.where(paired, 1.0, 0.0)

    matrix = system[...]
    first = matrix.astype(bf16)
    rest = matrix - first.astype(f32)
    second = rest.astype(bf16)
    high[...] = first
    mid[...] = second
    low[...] = (rest - second.astype(f32)).astype(bf16)
    down = 1.0 / jnp.sum(jnp.where(eye, matrix, 0.0), axis=1, keepdims=True)
    across = 1.0 / jnp.sum(jnp.where(eye, matrix, 0.0), axis=0, keepdims=True)
    guess_ref[...] = jnp.where(eye, 2.0 * across, 0.0) - down * matrix * across

    def going(state):
        step, error = state
        return (step < newton_steps) & jnp.logical_not(error <= newton_goal)

    def newton(state):
        guess = guess_ref[...]
        short = guess.astype(bf16)
        miss = jnp.where(eye, 1.0, 0.0) - jnp.dot(high[...], short, preferred_element_type=f32)
        better = guess + jnp.dot(short, miss.astype(bf16), preferred_element_type=f32)
        guess_ref[...] = better
        inverse[...] = better.astype(bf16)
        return state[0] + 1, jnp.sum(miss * miss)

    lax.while_loop(going, newton, newton((jnp.int32(0), jnp.float32(0.0))))


def solve_kernel(
    ta_count, swaps, own, far, system, high, mid, low, inverse, rows_out, low_out, exact
):
    frames, rank = rows_out.shape
    if swaps:
        rhs = own[0:frames, :]
        for k in range(1, ta_count):
            rhs = rhs + far[(k - 1) * frames : k * frames, :]
    else:
        rhs = far[0:frames, :]
        for k in range(1, ta_count):
            rhs = rhs + far[k * frames : (k + 1) * frames, :]
    dot = functools.partial(jnp.dot, preferred_element_type=f32)

    def residual(rows):
        one = rows.astype(bf16)
        rest = rows - one.astype(f32)
        two = rest.astype(bf16)
        three = (rest - two.astype(f32)).astype(bf16)
        a = dot(jnp.concatenate([one, two, three], axis=0), high[...])
        b = dot(jnp.concatenate([one, two], axis=0), mid[...])
        c = dot(one, low[...])
        small = (a[2 * frames :] + b[frames:]) + c
        return ((rhs - a[:frames]) - (a[frames : 2 * frames] + b[:frames])) - small

    rows = dot(rhs.astype(bf16), inverse[...])
    rest_a = residual(rows)
    rows = rows + dot(rest_a.astype(bf16), inverse[...])
    rest_b = residual(rows)
    rows = rows + dot(rest_b.astype(bf16), inverse[...])
    rows_out[...] = rows
    scale = 1.0 / jnp.maximum(jnp.sum(rhs * rhs), 1e-30)
    size_a = jnp.sum(rest_a * rest_a) * scale
    size_b = jnp.sum(rest_b * rest_b) * scale

    @pl.when(jnp.logical_not(size_b * size_b <= solve_goal * solve_goal * size_a))
    def _():
        exact[...] = system[...]
        lanes = lax.broadcasted_iota(jnp.int32, (1, rank), 1)
        subs = lax.broadcasted_iota(jnp.int32, (rank, 1), 0)

        @pl.loop(0, rank)
        def _(k):
            whole = exact[...]
            row = exact[pl.ds(k, 1), :]
            column = jnp.sum(jnp.where(lanes == k, whole, 0.0), axis=1, keepdims=True)
            pivot = 1.0 / jnp.sum(jnp.where(lanes == k, row, 0.0), axis=1, keepdims=True)
            scaled = jnp.where(lanes == k, 1.0, row) * pivot
            rest = jnp.where(lanes == k, 0.0, whole) - column * scaled
            exact[...] = jnp.where(subs == k, scaled, rest)

        full = functools.partial(dot, precision=top)
        answer = full(rhs, exact[...])
        miss = rhs - full(answer, system[...])
        rows_out[...] = answer + full(miss, exact[...])

    low_out[...] = rows_out[...].astype(bf16)


def misfit_kernel(ta_count, edge, swaps, table, low, far, full_z, full_y, cube, out, every):
    slots, frames = cube.shape[0], cube.shape[1]
    if swaps:
        every[0] = low[...].astype(f32)
    first = 1 if swaps else 0
    for k in range(first, ta_count):
        every[k] = far[(k - first) * frames : (k + 1 - first) * frames, :].astype(f32)
    me = lax.axis_index("ta")
    chunk = 8
    rank = full_z.shape[1]
    lane = lax.broadcasted_iota(jnp.int32, out.shape, 1)
    answer = jnp.zeros(out.shape, f32)
    over = (((1,), (1,)), ((), ()))
    for s in range(slots):
        at = pl.multiple_of(table[slots + s] * edge, edge)
        panel_z = full_z[pl.ds(at, edge), :].astype(f32)
        at = pl.multiple_of(table[2 * slots + s] * edge, edge)
        panel_y = full_y[pl.ds(at, edge), :]
        u = table[s]
        k = distance(u, me, swaps)
        total = jnp.zeros((8, edge), f32)
        for f in range(0, frames, chunk):
            rows = every[k, f : f + chunk, :]
            outer = (rows[:, None, :] * panel_z[None]).astype(bf16).reshape(chunk * edge, rank)
            model = lax.dot_general(outer, panel_y, over, preferred_element_type=f32)
            off = cube[s, f : f + chunk].reshape(chunk * edge, edge).astype(f32) - model
            total = total + jnp.sum((off * off).reshape(chunk * edge // 8, 8, edge), axis=0)
        mean = jnp.sum(total) * (1.0 / (frames * edge * edge))
        answer = jnp.where((lane == s) & (u >= 0), mean, answer)
    out[...] = answer


def swap(x, axis, count, k):
    return lax.ppermute(x, axis, [(i, i ^ k) for i in range(count)])


def body(blocks, qz_factor, qy_factor, block_owner, block_cells):
    ta_count, pb_count = lax.axis_size("ta"), lax.axis_size("pb")
    slots, frames, edge = blocks.shape[2], blocks.shape[3], blocks.shape[4]
    rows, rank = qz_factor.shape
    half, quarter = rows // 2, rows // 4
    swaps = (
        ta_count in (4, swap_limit) and pb_count % 4 == 0 and rows % 64 == 0
    )
    shape = jax.ShapeDtypeStruct
    cells = jnp.swapaxes(block_cells, 2, 3)
    full = [shape((ta_count * rows, rank), bf16)] * 2
    grid = ta_count * rows // edge

    def load(blocks, tables, infos):
        return pl.pallas_call(
            functools.partial(load_kernel, [grid] + tables),
            out_shape=[
                shape((slots, frames, edge, edge), bf16),
                shape((ta_count * slots + 2,), jnp.int32),
            ],
            in_specs=[hbm_spec] + [vmem_spec] * len(infos),
            out_specs=[vmem_spec, smem_spec],
            scratch_shapes=[pltpu.SemaphoreType.DMA((slots,))],
            compiler_params=params(8),
            cost_estimate=pl.CostEstimate(
                flops=0, transcendentals=0, bytes_accessed=4 * slots * frames * edge * edge
            ),
            name="load",
        )(held(blocks), *infos)

    if swaps:
        near, part, rest, table = pl.pallas_call(
            pack_kernel,
            out_shape=[
                shape((2 * half + info_rows, rank), bf16),
                shape((2 * quarter + info_rows, rank), bf16),
                shape((2 * half, rank), bf16),
                shape((3 * slots,), jnp.int32),
            ],
            in_specs=[hbm_spec] * 4,
            out_specs=[vmem_spec] * 3 + [smem_spec],
            scratch_shapes=[
                pltpu.SMEM(block_owner.shape, jnp.int32),
                pltpu.SMEM(cells.shape, jnp.int32),
                pltpu.SemaphoreType.DMA((8,)),
            ],
            compiler_params=params(4),
            name="pack",
        )(*(held(x) for x in (block_owner, cells, qz_factor, qy_factor)))
        first = swap(near, "ta", ta_count, 1)
        away = jnp.concatenate([swap(part, "ta", ta_count, k) for k in range(2, ta_count)], axis=0)
        first, away, blocks = lax.optimization_barrier((first, away, blocks))
        short = 2 * quarter + info_rows
        tables = [(0, 2 * half), (1, 2 * half)]
        tables += [(2, i * short + 2 * quarter) for i in range(ta_count - 2)]
        side_away, mate, (cube, found) = lax.optimization_barrier(
            (
                swap(away, "pb", pb_count, 2),
                swap(jnp.concatenate([first, away], axis=0), "pb", pb_count, 1),
                load(blocks, tables, (near, first, away)),
            )
        )
        side_mate = swap(side_away, "pb", pb_count, 1)
        pieces = (near, rest, first, away, side_away, mate, side_mate)
        made = full
    else:
        table = jnp.concatenate([block_owner.reshape(slots), cells.reshape(2 * slots)])
        pieces = (
            lax.all_gather(qz_factor, "ta", axis=0, tiled=True),
            lax.all_gather(qy_factor, "ta", axis=0, tiled=True),
        )
        made = []
        shown = jnp.zeros((info_rows, rank), jnp.int32)
        shown = shown.at[0, :slots].set(table[:slots] + 1)
        shown = shown.at[1:3, :slots].set(table[slots:].reshape(2, slots))
        info = lax.all_gather(shown.astype(bf16), "ta", axis=0, tiled=True)
        cube, found = load(blocks, [(0, k * info_rows) for k in range(ta_count)], (info,))
    out = pl.pallas_call(
        functools.partial(term_kernel, ta_count, edge, swaps),
        out_shape=[shape((ta_count * frames, rank), f32)] + made,
        in_specs=[smem_spec] + [vmem_spec] * (1 + len(pieces)),
        out_specs=[vmem_spec] * (1 + len(made)),
        compiler_params=params(16),
        name="terms",
    )(table, cube, *pieces)
    terms = out[0]
    if swaps:
        full_z, full_y = out[1:]
        arrived = jnp.concatenate(
            [
                swap(terms[k * frames : (k + 1) * frames], "ta", ta_count, k)
                for k in range(1, ta_count)
            ],
            axis=0,
        )
    else:
        full_z, full_y = pieces
        arrived = lax.all_to_all(terms, "ta", split_axis=0, concat_axis=0, tiled=True)
    square = [shape((rank, rank), f32)] + [shape((rank, rank), bf16)] * 4
    parts = pl.pallas_call(
        functools.partial(system_kernel, edge),
        out_shape=square,
        in_specs=[smem_spec] + [vmem_spec] * 2,
        out_specs=[vmem_spec] * 5,
        scratch_shapes=[pltpu.VMEM((rank, rank), f32)],
        compiler_params=params(16),
        name="system",
    )(found, full_z, full_y)
    new_rows, low = pl.pallas_call(
        functools.partial(solve_kernel, ta_count, swaps),
        out_shape=[shape((frames, rank), f32), shape((frames, rank), bf16)],
        in_specs=[vmem_spec] * 7,
        out_specs=[vmem_spec] * 2,
        scratch_shapes=[pltpu.VMEM((rank, rank), f32)],
        compiler_params=params(8),
        name="solve",
    )(terms, arrived, *parts)
    if swaps:
        others = jnp.concatenate([swap(low, "ta", ta_count, k) for k in range(1, ta_count)], axis=0)
    else:
        others = lax.all_gather(low, "ta", axis=0, tiled=True)
    misfit = pl.pallas_call(
        functools.partial(misfit_kernel, ta_count, edge, swaps),
        out_shape=shape((1, slots), f32),
        in_specs=[smem_spec] + [vmem_spec] * 5,
        out_specs=vmem_spec,
        scratch_shapes=[pltpu.VMEM((ta_count, frames, rank), f32)],
        compiler_params=params(16),
        name="misfit",
    )(table, low, others, full_z, full_y, cube)
    return (new_rows, misfit.reshape(1, 1, slots))


def solution(mesh):
    placed = (
        P(("series", "ta"), "pb", None, None, None, None),
        P(("series", "ta"), None),
        P(("series", "ta"), None),
        P(("series", "ta"), "pb", None),
        P(("series", "ta"), "pb", None, None),
    )
    return jax.shard_map(
        body,
        mesh=mesh,
        in_specs=placed,
        out_specs=(P(("series", "ta", "pb"), None), P(("series", "ta"), "pb", None)),
        check_vma=False,
    )
```

```python
import functools

import jax
import jax.numpy as jnp
from jax import lax
from jax.experimental import pallas as pl
from jax.experimental.pallas import tpu as pltpu
from jax.sharding import PartitionSpec as P


ridge_weight = 0.1
info_rows = 16
swap_limit = 8
newton_steps = 10
newton_goal = 0.25
solve_goal = 1e-3
top = lax.Precision.HIGHEST
f32 = jnp.float32
bf16 = jnp.bfloat16

vmem_spec = pl.BlockSpec(memory_space=pltpu.VMEM)
smem_spec = pl.BlockSpec(memory_space=pltpu.SMEM)
hbm_spec = pl.BlockSpec(memory_space=pltpu.HBM)


def held(x):
    return pltpu.with_memory_space_constraint(x, pltpu.HBM)


def params(mib):
    return pltpu.CompilerParams(vmem_limit_bytes=mib * 1024 * 1024)


def pack_kernel(owner_hbm, cells_hbm, z_hbm, y_hbm, half_ref, part_ref, rest_ref, table_ref, owner, cells, sems):
    half = z_hbm.shape[0] // 2
    part = half // 2
    rank = z_hbm.shape[1]
    slots = owner.shape[2]
    column = lax.axis_index("pb")
    core = lax.rem(column, 2)
    side = lax.rem(lax.div(column, 2), 2)
    small = [
        pltpu.make_async_copy(owner_hbm, owner, sems.at[6]),
        pltpu.make_async_copy(cells_hbm, cells, sems.at[7]),
    ]
    copies = []
    pieces = (
        (half_ref, core * half, half),
        (part_ref, core * half + side * part, part),
        (rest_ref, (1 - core) * half, half),
    )
    for i, (target, at, count) in enumerate(pieces):
        for j, source in enumerate((z_hbm, y_hbm)):
            copies.append(
                pltpu.make_async_copy(
                    source.at[pl.ds(pl.multiple_of(at, count), count), :],
                    target.at[j * count : (j + 1) * count, :],
                    sems.at[2 * i + j],
                )
            )
    for copy in small + copies:
        copy.start()
    for copy in small:
        copy.wait()
    shape = (info_rows, rank)
    row = lax.broadcasted_iota(jnp.int32, shape, 0)
    lane = lax.broadcasted_iota(jnp.int32, shape, 1)
    table = jnp.zeros(shape, jnp.int32)
    for s in range(slots):
        values = (owner[0, 0, s], cells[0, 0, 0, s], cells[0, 0, 1, s])
        for r, value in enumerate(values):
            table_ref[r * slots + s] = value
            shown = value + 1 if r == 0 else value
            table = jnp.where((row == r) & (lane == s), shown, table)
    table = table.astype(f32).astype(bf16)
    half_ref[2 * half :, :] = table
    part_ref[2 * part :, :] = table
    for copy in copies:
        copy.wait()


def distance(u, me, swaps):
    u = jnp.maximum(u, 0)
    return lax.bitwise_xor(u, me) if swaps else u


def load_kernel(tables, blocks, *refs):
    infos, (cube, found, sems) = refs[:-3], refs[-3:]
    slots = cube.shape[0]
    copies = [pltpu.make_async_copy(blocks.at[0, 0, s], cube.at[s], sems.at[s]) for s in range(slots)]
    for copy in copies:
        copy.start()
    rank = infos[0].shape[1]
    me = lax.axis_index("ta")
    grid = tables[0]
    lane = lax.broadcasted_iota(jnp.int32, (1, rank), 1)
    codes = []
    for which, base in tables[1:]:
        table = infos[which][base : base + info_rows, :].astype(f32)
        cell = (table[1:2, :] * grid + table[2:3, :]).astype(jnp.int32)
        wanted = table[0:1, :].astype(jnp.int32) == me + 1
        code = jnp.where(wanted, cell, -1)
        codes += [jnp.max(jnp.where(lane == s, code, -1)) for s in range(slots)]
    count = jnp.int32(0)
    for code in codes:
        found[1 + count] = code
        count = count + (code >= 0).astype(jnp.int32)
    found[0] = count
    for copy in copies:
        copy.wait()


def assemble(near, rest, first, away, side_away, mate, side_mate, full_z, full_y):
    half = rest.shape[0] // 2
    quarter = half // 2
    rows = 2 * half
    tall = 2 * half + info_rows
    short = 2 * quarter + info_rows
    me = lax.axis_index("ta")
    column = lax.axis_index("pb")
    core = lax.rem(column, 2)
    side = lax.rem(lax.div(column, 2), 2)

    def put(ref, base, at, count):
        at = pl.ds(pl.multiple_of(at, count), count)
        full_z[at, :] = ref[base : base + count, :]
        full_y[at, :] = ref[base + count : base + 2 * count, :]

    put(near, 0, me * rows + core * half, half)
    put(rest, 0, me * rows + (1 - core) * half, half)
    source = lax.bitwise_xor(me, 1) * rows
    put(first, 0, source + core * half, half)
    put(mate, 0, source + (1 - core) * half, half)
    others = away.shape[0] // short
    for i in range(others):
        source = lax.bitwise_xor(me, i + 2) * rows
        base = i * short
        for ref, start, which, where in (
            (away, 0, core, side),
            (side_away, 0, core, 1 - side),
            (mate, tall, 1 - core, side),
            (side_mate, 0, 1 - core, 1 - side),
        ):
            put(ref, start + base, source + which * half + where * quarter, quarter)


def term_kernel(edge, swaps, table, cube, *refs):
    if swaps:
        pieces, (terms, full_z, full_y) = refs[:-3], refs[-3:]
        assemble(*pieces, full_z, full_y)
    else:
        full_z, full_y, terms = refs
    slots, frames = cube.shape[0], cube.shape[1]
    me = lax.axis_index("ta")
    terms[...] = jnp.zeros_like(terms)
    chunk = 8
    rank = full_z.shape[1]
    for s in range(slots):
        at = pl.multiple_of(table[slots + s] * edge, edge)
        panel_z = full_z[pl.ds(at, edge), :].astype(f32)
        at = pl.multiple_of(table[2 * slots + s] * edge, edge)
        panel_y = full_y[pl.ds(at, edge), :]
        u = table[s]
        live = u >= 0
        k = distance(u, me, swaps)
        for f in range(0, frames, chunk):
            part = cube[s, f : f + chunk].reshape(chunk * edge, edge)
            inner = jnp.dot(part, panel_y, preferred_element_type=f32)
            summed = jnp.sum(inner.reshape(chunk, edge, rank) * panel_z[None], axis=1)
            at = pl.ds(pl.multiple_of(k * frames + f, chunk), chunk)
            terms[at, :] += jnp.where(live, summed, 0.0)


def system_kernel(edge, found, full_z, full_y, system, high, mid, low, inverse, tail, guess_ref):
    rank = full_z.shape[1]
    grid = full_z.shape[0] // edge
    count = found[0]
    eye = lax.broadcasted_iota(jnp.int32, (rank, rank), 0) == lax.broadcasted_iota(
        jnp.int32, (rank, rank), 1
    )
    system[...] = jnp.where(eye, ridge_weight, 0.0).astype(f32)

    def product(code):
        over = (((0,), (0,)), ((), ()))
        at = pl.multiple_of(lax.div(code, grid) * edge, edge)
        panel_z = full_z[pl.ds(at, edge), :]
        at = pl.multiple_of(lax.rem(code, grid) * edge, edge)
        panel_y = full_y[pl.ds(at, edge), :]
        gram_z = lax.dot_general(panel_z, panel_z, over, preferred_element_type=f32)
        gram_y = lax.dot_general(panel_y, panel_y, over, preferred_element_type=f32)
        return gram_z * gram_y

    @pl.loop(0, lax.div(count + 1, 2))
    def _(j):
        one = found[1 + 2 * j]
        paired = 2 * j + 1 < count
        two = jnp.where(paired, found[2 + 2 * j], one)
        system[...] += product(one) + product(two) * jnp.where(paired, 1.0, 0.0)

    matrix = system[...]
    first = matrix.astype(bf16)
    rest = matrix - first.astype(f32)
    second = rest.astype(bf16)
    high[...] = first
    mid[...] = second
    low[...] = (rest - second.astype(f32)).astype(bf16)
    down = 1.0 / jnp.sum(jnp.where(eye, matrix, 0.0), axis=1, keepdims=True)
    across = 1.0 / jnp.sum(jnp.where(eye, matrix, 0.0), axis=0, keepdims=True)
    guess_ref[...] = jnp.where(eye, 2.0 * across, 0.0) - down * matrix * across

    unit = jnp.where(eye, 1.0, 0.0)
    dot = functools.partial(jnp.dot, preferred_element_type=f32)

    def going(state):
        step, error = state
        return (step < newton_steps) & jnp.logical_not(error <= newton_goal)

    def newton(state):
        guess = guess_ref[...]
        short = guess.astype(bf16)
        miss = unit - dot(high[...], short)
        guess_ref[...] = guess + dot(short, miss.astype(bf16))
        return state[0] + 1, jnp.sum(miss * miss)

    lax.while_loop(going, newton, newton((jnp.int32(0), jnp.float32(0.0))))
    guess = guess_ref[...]
    short = guess.astype(bf16)
    rest = (guess - short.astype(f32)).astype(bf16)
    miss = (unit - dot(high[...], short)) - (dot(high[...], rest) + dot(mid[...], short))
    better = guess + dot(short, miss.astype(bf16))
    short = better.astype(bf16)
    inverse[...] = short
    tail[...] = (better - short.astype(f32)).astype(bf16)


def solve_kernel(
    ta_count, swaps, own, far, system, high, mid, low, inverse, tail, rows_out, low_out, exact
):
    frames, rank = rows_out.shape
    if swaps:
        rhs = own[0:frames, :]
        for k in range(1, ta_count):
            rhs = rhs + far[(k - 1) * frames : k * frames, :]
    else:
        rhs = far[0:frames, :]
        for k in range(1, ta_count):
            rhs = rhs + far[k * frames : (k + 1) * frames, :]
    dot = functools.partial(jnp.dot, preferred_element_type=f32)

    def residual(rows):
        one = rows.astype(bf16)
        rest = rows - one.astype(f32)
        two = rest.astype(bf16)
        three = (rest - two.astype(f32)).astype(bf16)
        a = dot(jnp.concatenate([one, two, three], axis=0), high[...])
        b = dot(jnp.concatenate([one, two], axis=0), mid[...])
        c = dot(one, low[...])
        small = (a[2 * frames :] + b[frames:]) + c
        return ((rhs - a[:frames]) - (a[frames : 2 * frames] + b[:frames])) - small

    def solved(right):
        one = right.astype(bf16)
        two = (right - one.astype(f32)).astype(bf16)
        a = dot(jnp.concatenate([one, two], axis=0), inverse[...])
        return a[:frames] + (a[frames:] + dot(one, tail[...]))

    rows = solved(rhs)
    rest = residual(rows)
    rows = rows + solved(rest)
    rows_out[...] = rows
    low_out[...] = rows.astype(bf16)

    @pl.when(
        jnp.logical_not(jnp.sum(rest * rest) <= solve_goal * solve_goal * jnp.sum(rhs * rhs))
    )
    def _():
        exact[...] = system[...]
        lanes = lax.broadcasted_iota(jnp.int32, (1, rank), 1)
        subs = lax.broadcasted_iota(jnp.int32, (rank, 1), 0)

        @pl.loop(0, rank)
        def _(k):
            whole = exact[...]
            row = exact[pl.ds(k, 1), :]
            column = jnp.sum(jnp.where(lanes == k, whole, 0.0), axis=1, keepdims=True)
            pivot = 1.0 / jnp.sum(jnp.where(lanes == k, row, 0.0), axis=1, keepdims=True)
            scaled = jnp.where(lanes == k, 1.0, row) * pivot
            rest = jnp.where(lanes == k, 0.0, whole) - column * scaled
            exact[...] = jnp.where(subs == k, scaled, rest)

        full = functools.partial(dot, precision=top)
        answer = full(rhs, exact[...])
        miss = rhs - full(answer, system[...])
        answer = answer + full(miss, exact[...])
        rows_out[...] = answer
        low_out[...] = answer.astype(bf16)


def misfit_kernel(ta_count, edge, swaps, table, low, far, full_z, full_y, cube, out, every):
    slots, frames = cube.shape[0], cube.shape[1]
    if swaps:
        every[0] = low[...].astype(f32)
    first = 1 if swaps else 0
    for k in range(first, ta_count):
        every[k] = far[(k - first) * frames : (k + 1 - first) * frames, :].astype(f32)
    me = lax.axis_index("ta")
    chunk = 8
    rank = full_z.shape[1]
    lane = lax.broadcasted_iota(jnp.int32, out.shape, 1)
    answer = jnp.zeros(out.shape, f32)
    over = (((1,), (1,)), ((), ()))
    for s in range(slots):
        at = pl.multiple_of(table[slots + s] * edge, edge)
        panel_z = full_z[pl.ds(at, edge), :].astype(f32)
        at = pl.multiple_of(table[2 * slots + s] * edge, edge)
        panel_y = full_y[pl.ds(at, edge), :]
        u = table[s]
        k = distance(u, me, swaps)
        total = jnp.zeros((8, edge), f32)
        for f in range(0, frames, chunk):
            rows = every[k, f : f + chunk, :]
            outer = (rows[:, None, :] * panel_z[None]).astype(bf16).reshape(chunk * edge, rank)
            model = lax.dot_general(outer, panel_y, over, preferred_element_type=f32)
            off = cube[s, f : f + chunk].reshape(chunk * edge, edge).astype(f32) - model
            total = total + jnp.sum((off * off).reshape(chunk * edge // 8, 8, edge), axis=0)
        mean = jnp.sum(total) * (1.0 / (frames * edge * edge))
        answer = jnp.where((lane == s) & (u >= 0), mean, answer)
    out[...] = answer


def swap(x, axis, count, k):
    return lax.ppermute(x, axis, [(i, i ^ k) for i in range(count)])


def body(blocks, qz_factor, qy_factor, block_owner, block_cells):
    ta_count, pb_count = lax.axis_size("ta"), lax.axis_size("pb")
    slots, frames, edge = blocks.shape[2], blocks.shape[3], blocks.shape[4]
    rows, rank = qz_factor.shape
    half, quarter = rows // 2, rows // 4
    swaps = (
        ta_count in (4, swap_limit) and pb_count % 4 == 0 and rows % 64 == 0
    )
    shape = jax.ShapeDtypeStruct
    cells = jnp.swapaxes(block_cells, 2, 3)
    full = [shape((ta_count * rows, rank), bf16)] * 2
    grid = ta_count * rows // edge

    def load(blocks, tables, infos):
        return pl.pallas_call(
            functools.partial(load_kernel, [grid] + tables),
            out_shape=[
                shape((slots, frames, edge, edge), bf16),
                shape((ta_count * slots + 2,), jnp.int32),
            ],
            in_specs=[hbm_spec] + [vmem_spec] * len(infos),
            out_specs=[vmem_spec, smem_spec],
            scratch_shapes=[pltpu.SemaphoreType.DMA((slots,))],
            compiler_params=params(8),
            cost_estimate=pl.CostEstimate(
                flops=0, transcendentals=0, bytes_accessed=4 * slots * frames * edge * edge
            ),
            name="load",
        )(held(blocks), *infos)

    if swaps:
        near, part, rest, table = pl.pallas_call(
            pack_kernel,
            out_shape=[
                shape((2 * half + info_rows, rank), bf16),
                shape((2 * quarter + info_rows, rank), bf16),
                shape((2 * half, rank), bf16),
                shape((3 * slots,), jnp.int32),
            ],
            in_specs=[hbm_spec] * 4,
            out_specs=[vmem_spec] * 3 + [smem_spec],
            scratch_shapes=[
                pltpu.SMEM(block_owner.shape, jnp.int32),
                pltpu.SMEM(cells.shape, jnp.int32),
                pltpu.SemaphoreType.DMA((8,)),
            ],
            compiler_params=params(4),
            name="pack",
        )(*(held(x) for x in (block_owner, cells, qz_factor, qy_factor)))
        first = swap(near, "ta", ta_count, 1)
        away = jnp.concatenate([swap(part, "ta", ta_count, k) for k in range(2, ta_count)], axis=0)
        first, away, blocks = lax.optimization_barrier((first, away, blocks))
        short = 2 * quarter + info_rows
        tables = [(0, 2 * half), (1, 2 * half)]
        tables += [(2, i * short + 2 * quarter) for i in range(ta_count - 2)]
        both = jnp.concatenate([first, away], axis=0)
        cube, found = load(blocks, tables, (near, first, away))
        both, cube, found = lax.optimization_barrier((both, cube, found))
        side_away, mate = lax.optimization_barrier(
            (swap(away, "pb", pb_count, 2), swap(both, "pb", pb_count, 1))
        )
        side_mate = swap(side_away, "pb", pb_count, 1)
        pieces = (near, rest, first, away, side_away, mate, side_mate)
        made = full
    else:
        table = jnp.concatenate([block_owner.reshape(slots), cells.reshape(2 * slots)])
        pieces = (
            lax.all_gather(qz_factor, "ta", axis=0, tiled=True),
            lax.all_gather(qy_factor, "ta", axis=0, tiled=True),
        )
        made = []
        shown = jnp.zeros((info_rows, rank), jnp.int32)
        shown = shown.at[0, :slots].set(table[:slots] + 1)
        shown = shown.at[1:3, :slots].set(table[slots:].reshape(2, slots))
        info = lax.all_gather(shown.astype(bf16), "ta", axis=0, tiled=True)
        cube, found = load(blocks, [(0, k * info_rows) for k in range(ta_count)], (info,))
    out = pl.pallas_call(
        functools.partial(term_kernel, edge, swaps),
        out_shape=[shape((ta_count * frames, rank), f32)] + made,
        in_specs=[smem_spec] + [vmem_spec] * (1 + len(pieces)),
        out_specs=[vmem_spec] * (1 + len(made)),
        compiler_params=params(16),
        name="terms",
    )(table, cube, *pieces)
    terms = out[0]
    if swaps:
        full_z, full_y = out[1:]
        arrived = jnp.concatenate(
            [
                swap(terms[k * frames : (k + 1) * frames], "ta", ta_count, k)
                for k in range(1, ta_count)
            ],
            axis=0,
        )
    else:
        full_z, full_y = pieces
        arrived = lax.all_to_all(terms, "ta", split_axis=0, concat_axis=0, tiled=True)
    square = [shape((rank, rank), f32)] + [shape((rank, rank), bf16)] * 5
    parts = pl.pallas_call(
        functools.partial(system_kernel, edge),
        out_shape=square,
        in_specs=[smem_spec] + [vmem_spec] * 2,
        out_specs=[vmem_spec] * 6,
        scratch_shapes=[pltpu.VMEM((rank, rank), f32)],
        compiler_params=params(16),
        name="system",
    )(found, full_z, full_y)
    new_rows, low = pl.pallas_call(
        functools.partial(solve_kernel, ta_count, swaps),
        out_shape=[shape((frames, rank), f32), shape((frames, rank), bf16)],
        in_specs=[vmem_spec] * 8,
        out_specs=[vmem_spec] * 2,
        scratch_shapes=[pltpu.VMEM((rank, rank), f32)],
        compiler_params=params(8),
        name="solve",
    )(terms, arrived, *parts)
    if swaps:
        others = jnp.concatenate([swap(low, "ta", ta_count, k) for k in range(1, ta_count)], axis=0)
    else:
        others = lax.all_gather(low, "ta", axis=0, tiled=True)
    misfit = pl.pallas_call(
        functools.partial(misfit_kernel, ta_count, edge, swaps),
        out_shape=shape((1, slots), f32),
        in_specs=[smem_spec] + [vmem_spec] * 5,
        out_specs=vmem_spec,
        scratch_shapes=[pltpu.VMEM((ta_count, frames, rank), f32)],
        compiler_params=params(16),
        name="misfit",
    )(table, low, others, full_z, full_y, cube)
    return (new_rows, misfit.reshape(1, 1, slots))


def solution(mesh):
    placed = (
        P(("series", "ta"), "pb", None, None, None, None),
        P(("series", "ta"), None),
        P(("series", "ta"), None),
        P(("series", "ta"), "pb", None),
        P(("series", "ta"), "pb", None, None),
    )

    return jax.shard_map(
        body,
        mesh=mesh,
        in_specs=placed,
        out_specs=(P(("series", "ta", "pb"), None), P(("series", "ta"), "pb", None)),
        check_vma=False,
    )
```

```python
import functools

import jax
import jax.numpy as jnp
from jax import lax
from jax.experimental import pallas as pl
from jax.experimental.pallas import tpu as pltpu
from jax.sharding import PartitionSpec as P


ridge_weight = 0.1
info_rows = 8
swap_limit = 8
newton_steps = 10
newton_goal = 0.25
solve_goal = 1e-3
top = lax.Precision.HIGHEST
f32 = jnp.float32
bf16 = jnp.bfloat16

vmem_spec = pl.BlockSpec(memory_space=pltpu.VMEM)
smem_spec = pl.BlockSpec(memory_space=pltpu.SMEM)
hbm_spec = pl.BlockSpec(memory_space=pltpu.HBM)


def held(x):
    return pltpu.with_memory_space_constraint(x, pltpu.HBM)


def params(mib):
    return pltpu.CompilerParams(vmem_limit_bytes=mib * 1024 * 1024)


def pack_kernel(owner_hbm, cells_hbm, z_hbm, y_hbm, half_ref, part_ref, rest_ref, owner, cells, sems):
    half = z_hbm.shape[0] // 2
    part = half // 2
    rank = z_hbm.shape[1]
    slots = owner.shape[2]
    column = lax.axis_index("pb")
    core = lax.rem(column, 2)
    side = lax.rem(lax.div(column, 2), 2)
    small = [
        pltpu.make_async_copy(owner_hbm, owner, sems.at[6]),
        pltpu.make_async_copy(cells_hbm, cells, sems.at[7]),
    ]
    copies = []
    pieces = (
        (half_ref, core * half, half),
        (part_ref, core * half + side * part, part),
        (rest_ref, (1 - core) * half, half),
    )
    for i, (target, at, count) in enumerate(pieces):
        for j, source in enumerate((z_hbm, y_hbm)):
            copies.append(
                pltpu.make_async_copy(
                    source.at[pl.ds(pl.multiple_of(at, count), count), :],
                    target.at[j * count : (j + 1) * count, :],
                    sems.at[2 * i + j],
                )
            )
    for copy in small + copies:
        copy.start()
    for copy in small:
        copy.wait()
    shape = (info_rows, rank)
    row = lax.broadcasted_iota(jnp.int32, shape, 0)
    lane = lax.broadcasted_iota(jnp.int32, shape, 1)
    table = jnp.zeros(shape, jnp.int32)
    for s in range(slots):
        values = (owner[0, 0, s], cells[0, 0, 0, s], cells[0, 0, 1, s])
        for r, value in enumerate(values):
            shown = value + 1 if r == 0 else value
            table = jnp.where((row == r) & (lane == s), shown, table)
    table = table.astype(f32).astype(bf16)
    half_ref[2 * half :, :] = table
    part_ref[2 * part :, :] = table
    for copy in copies:
        copy.wait()


def distance(u, me, swaps):
    u = jnp.maximum(u, 0)
    return lax.bitwise_xor(u, me) if swaps else u


def load_kernel(blocks, owner_hbm, cells_hbm, cube, table, owner, cells, sems):
    slots = cube.shape[0]
    copies = [
        pltpu.make_async_copy(owner_hbm, owner, sems.at[slots]),
        pltpu.make_async_copy(cells_hbm, cells, sems.at[slots + 1]),
    ]
    copies += [
        pltpu.make_async_copy(blocks.at[0, 0, s], cube.at[s], sems.at[s]) for s in range(slots)
    ]
    for copy in copies:
        copy.start()
    for copy in copies:
        copy.wait()
    for s in range(slots):
        table[s] = owner[0, 0, s]
        table[slots + s] = cells[0, 0, 0, s]
        table[2 * slots + s] = cells[0, 0, 1, s]


def match_kernel(slots, grid, tables, *refs):
    infos, found = refs[:-1], refs[-1]
    rank = infos[0].shape[1]
    me = lax.axis_index("ta")
    lane = lax.broadcasted_iota(jnp.int32, (1, rank), 1)
    codes = []
    for which, base in tables:
        table = infos[which][base : base + info_rows, :].astype(f32)
        cell = (table[1:2, :] * grid + table[2:3, :]).astype(jnp.int32)
        wanted = table[0:1, :].astype(jnp.int32) == me + 1
        code = jnp.where(wanted, cell, -1)
        codes += [jnp.max(jnp.where(lane == s, code, -1)) for s in range(slots)]
    count = jnp.int32(0)
    for code in codes:
        found[1 + count] = code
        count = count + (code >= 0).astype(jnp.int32)
    found[0] = count


def assemble(near, rest, first, away, side_away, mate, side_mate, full_z, full_y):
    half = rest.shape[0] // 2
    quarter = half // 2
    rows = 2 * half
    tall = 2 * half
    short = 2 * quarter
    me = lax.axis_index("ta")
    column = lax.axis_index("pb")
    core = lax.rem(column, 2)
    side = lax.rem(lax.div(column, 2), 2)

    def put(ref, base, at, count):
        at = pl.ds(pl.multiple_of(at, count), count)
        full_z[at, :] = ref[base : base + count, :]
        full_y[at, :] = ref[base + count : base + 2 * count, :]

    put(near, 0, me * rows + core * half, half)
    put(rest, 0, me * rows + (1 - core) * half, half)
    source = lax.bitwise_xor(me, 1) * rows
    put(first, 0, source + core * half, half)
    put(mate, 0, source + (1 - core) * half, half)
    others = away.shape[0] // short
    for i in range(others):
        source = lax.bitwise_xor(me, i + 2) * rows
        base = i * short
        for ref, start, which, where in (
            (away, 0, core, side),
            (side_away, 0, core, 1 - side),
            (mate, tall, 1 - core, side),
            (side_mate, 0, 1 - core, 1 - side),
        ):
            put(ref, start + base, source + which * half + where * quarter, quarter)


def term_kernel(edge, swaps, table, cube, *refs):
    if swaps:
        pieces, (terms, full_z, full_y) = refs[:-3], refs[-3:]
        assemble(*pieces, full_z, full_y)
    else:
        full_z, full_y, terms = refs
    slots, frames = cube.shape[0], cube.shape[1]
    me = lax.axis_index("ta")
    terms[...] = jnp.zeros_like(terms)
    chunk = 8
    rank = full_z.shape[1]
    for s in range(slots):
        at = pl.multiple_of(table[slots + s] * edge, edge)
        panel_z = full_z[pl.ds(at, edge), :].astype(f32)
        at = pl.multiple_of(table[2 * slots + s] * edge, edge)
        panel_y = full_y[pl.ds(at, edge), :]
        u = table[s]
        live = u >= 0
        k = distance(u, me, swaps)
        for f in range(0, frames, chunk):
            part = cube[s, f : f + chunk].reshape(chunk * edge, edge)
            inner = jnp.dot(part, panel_y, preferred_element_type=f32)
            summed = jnp.sum(inner.reshape(chunk, edge, rank) * panel_z[None], axis=1)
            at = pl.ds(pl.multiple_of(k * frames + f, chunk), chunk)
            terms[at, :] += jnp.where(live, summed, 0.0)


def system_kernel(edge, found, full_z, full_y, system, high, mid, low, inverse, tail, guess_ref):
    rank = full_z.shape[1]
    grid = full_z.shape[0] // edge
    count = found[0]
    eye = lax.broadcasted_iota(jnp.int32, (rank, rank), 0) == lax.broadcasted_iota(
        jnp.int32, (rank, rank), 1
    )
    system[...] = jnp.where(eye, ridge_weight, 0.0).astype(f32)

    def product(code):
        over = (((0,), (0,)), ((), ()))
        at = pl.multiple_of(lax.div(code, grid) * edge, edge)
        panel_z = full_z[pl.ds(at, edge), :]
        at = pl.multiple_of(lax.rem(code, grid) * edge, edge)
        panel_y = full_y[pl.ds(at, edge), :]
        gram_z = lax.dot_general(panel_z, panel_z, over, preferred_element_type=f32)
        gram_y = lax.dot_general(panel_y, panel_y, over, preferred_element_type=f32)
        return gram_z * gram_y

    @pl.loop(0, lax.div(count + 1, 2))
    def _(j):
        one = found[1 + 2 * j]
        paired = 2 * j + 1 < count
        two = jnp.where(paired, found[2 + 2 * j], one)
        system[...] += product(one) + product(two) * jnp.where(paired, 1.0, 0.0)

    matrix = system[...]
    first = matrix.astype(bf16)
    rest = matrix - first.astype(f32)
    second = rest.astype(bf16)
    high[...] = first
    mid[...] = second
    low[...] = (rest - second.astype(f32)).astype(bf16)
    down = 1.0 / jnp.sum(jnp.where(eye, matrix, 0.0), axis=1, keepdims=True)
    across = 1.0 / jnp.sum(jnp.where(eye, matrix, 0.0), axis=0, keepdims=True)
    guess_ref[...] = jnp.where(eye, 2.0 * across, 0.0) - down * matrix * across

    unit = jnp.where(eye, 1.0, 0.0)
    dot = functools.partial(jnp.dot, preferred_element_type=f32)

    def going(state):
        step, error = state
        return (step < newton_steps) & jnp.logical_not(error <= newton_goal)

    def newton(state):
        guess = guess_ref[...]
        short = guess.astype(bf16)
        miss = unit - dot(high[...], short)
        guess_ref[...] = guess + dot(short, miss.astype(bf16))
        return state[0] + 1, jnp.sum(miss * miss)

    lax.while_loop(going, newton, newton((jnp.int32(0), jnp.float32(0.0))))
    guess = guess_ref[...]
    short = guess.astype(bf16)
    rest = (guess - short.astype(f32)).astype(bf16)
    miss = (unit - dot(high[...], short)) - (dot(high[...], rest) + dot(mid[...], short))
    better = guess + dot(short, miss.astype(bf16))
    short = better.astype(bf16)
    inverse[...] = short
    tail[...] = (better - short.astype(f32)).astype(bf16)


def solve_kernel(
    ta_count, swaps, own, far, system, high, mid, low, inverse, tail, rows_out, low_out, exact
):
    frames, rank = rows_out.shape
    if swaps:
        rhs = own[0:frames, :]
        for k in range(1, ta_count):
            rhs = rhs + far[(k - 1) * frames : k * frames, :]
    else:
        rhs = far[0:frames, :]
        for k in range(1, ta_count):
            rhs = rhs + far[k * frames : (k + 1) * frames, :]
    dot = functools.partial(jnp.dot, preferred_element_type=f32)

    def residual(rows):
        one = rows.astype(bf16)
        rest = rows - one.astype(f32)
        two = rest.astype(bf16)
        three = (rest - two.astype(f32)).astype(bf16)
        a = dot(jnp.concatenate([one, two, three], axis=0), high[...])
        b = dot(jnp.concatenate([one, two], axis=0), mid[...])
        c = dot(one, low[...])
        small = (a[2 * frames :] + b[frames:]) + c
        return ((rhs - a[:frames]) - (a[frames : 2 * frames] + b[:frames])) - small

    def solved(right):
        one = right.astype(bf16)
        two = (right - one.astype(f32)).astype(bf16)
        a = dot(jnp.concatenate([one, two], axis=0), inverse[...])
        return a[:frames] + (a[frames:] + dot(one, tail[...]))

    rows = solved(rhs)
    rest = residual(rows)
    rows = rows + solved(rest)
    rows_out[...] = rows
    low_out[...] = rows.astype(bf16)

    @pl.when(
        jnp.logical_not(jnp.sum(rest * rest) <= solve_goal * solve_goal * jnp.sum(rhs * rhs))
    )
    def _():
        exact[...] = system[...]
        lanes = lax.broadcasted_iota(jnp.int32, (1, rank), 1)
        subs = lax.broadcasted_iota(jnp.int32, (rank, 1), 0)

        @pl.loop(0, rank)
        def _(k):
            whole = exact[...]
            row = exact[pl.ds(k, 1), :]
            column = jnp.sum(jnp.where(lanes == k, whole, 0.0), axis=1, keepdims=True)
            pivot = 1.0 / jnp.sum(jnp.where(lanes == k, row, 0.0), axis=1, keepdims=True)
            scaled = jnp.where(lanes == k, 1.0, row) * pivot
            rest = jnp.where(lanes == k, 0.0, whole) - column * scaled
            exact[...] = jnp.where(subs == k, scaled, rest)

        full = functools.partial(dot, precision=top)
        answer = full(rhs, exact[...])
        miss = rhs - full(answer, system[...])
        answer = answer + full(miss, exact[...])
        rows_out[...] = answer
        low_out[...] = answer.astype(bf16)


def misfit_kernel(
    ta_count, edge, swaps, table, low, far, full_z, full_y, cube, rows_in, out, rows_out, every, sem
):
    slots, frames = cube.shape[0], cube.shape[1]
    leaving = pltpu.make_async_copy(rows_in, rows_out, sem)
    leaving.start()
    if swaps:
        every[0] = low[...].astype(f32)
    first = 1 if swaps else 0
    for k in range(first, ta_count):
        every[k] = far[(k - first) * frames : (k + 1 - first) * frames, :].astype(f32)
    me = lax.axis_index("ta")
    chunk = 8
    rank = full_z.shape[1]
    lane = lax.broadcasted_iota(jnp.int32, out.shape, 1)
    answer = jnp.zeros(out.shape, f32)
    over = (((1,), (1,)), ((), ()))
    for s in range(slots):
        at = pl.multiple_of(table[slots + s] * edge, edge)
        panel_z = full_z[pl.ds(at, edge), :].astype(f32)
        at = pl.multiple_of(table[2 * slots + s] * edge, edge)
        panel_y = full_y[pl.ds(at, edge), :]
        u = table[s]
        k = distance(u, me, swaps)
        total = jnp.zeros((8, edge), f32)
        for f in range(0, frames, chunk):
            rows = every[k, f : f + chunk, :]
            outer = (rows[:, None, :] * panel_z[None]).astype(bf16).reshape(chunk * edge, rank)
            model = lax.dot_general(outer, panel_y, over, preferred_element_type=f32)
            off = cube[s, f : f + chunk].reshape(chunk * edge, edge).astype(f32) - model
            total = total + jnp.sum((off * off).reshape(chunk * edge // 8, 8, edge), axis=0)
        mean = jnp.sum(total) * (1.0 / (frames * edge * edge))
        answer = jnp.where((lane == s) & (u >= 0), mean, answer)
    out[...] = answer
    leaving.wait()


def swap(x, axis, count, k):
    return lax.ppermute(x, axis, [(i, i ^ k) for i in range(count)])


def body(blocks, qz_factor, qy_factor, block_owner, block_cells):
    ta_count, pb_count = lax.axis_size("ta"), lax.axis_size("pb")
    slots, frames, edge = blocks.shape[2], blocks.shape[3], blocks.shape[4]
    rows, rank = qz_factor.shape
    half, quarter = rows // 2, rows // 4
    swaps = (
        ta_count in (4, swap_limit) and pb_count % 4 == 0 and rows % 64 == 0
    )
    shape = jax.ShapeDtypeStruct
    cells = jnp.swapaxes(block_cells, 2, 3)
    full = [shape((ta_count * rows, rank), bf16)] * 2
    grid = ta_count * rows // edge
    small = [
        pltpu.SMEM(block_owner.shape, jnp.int32),
        pltpu.SMEM(cells.shape, jnp.int32),
    ]
    cube, table = pl.pallas_call(
        load_kernel,
        out_shape=[
            shape((slots, frames, edge, edge), bf16),
            shape((3 * slots,), jnp.int32),
        ],
        in_specs=[hbm_spec] * 3,
        out_specs=[vmem_spec, smem_spec],
        scratch_shapes=small + [pltpu.SemaphoreType.DMA((slots + 2,))],
        compiler_params=params(8),
        cost_estimate=pl.CostEstimate(
            flops=0, transcendentals=0, bytes_accessed=4 * slots * frames * edge * edge
        ),
        name="load",
    )(held(blocks), held(block_owner), held(cells))

    def match(tables, infos):
        return pl.pallas_call(
            functools.partial(match_kernel, slots, grid, tables),
            out_shape=shape((ta_count * slots + 2,), jnp.int32),
            in_specs=[vmem_spec] * len(infos),
            out_specs=smem_spec,
            compiler_params=params(4),
            name="match",
        )(*infos)

    if swaps:
        near, part, rest = pl.pallas_call(
            pack_kernel,
            out_shape=[
                shape((2 * half + info_rows, rank), bf16),
                shape((2 * quarter + info_rows, rank), bf16),
                shape((2 * half, rank), bf16),
            ],
            in_specs=[hbm_spec] * 4,
            out_specs=[vmem_spec] * 3,
            scratch_shapes=small + [pltpu.SemaphoreType.DMA((8,))],
            compiler_params=params(4),
            name="pack",
        )(*(held(x) for x in (block_owner, cells, qz_factor, qy_factor)))
        first = swap(near, "ta", ta_count, 1)
        parts = [swap(part, "ta", ta_count, k) for k in range(2, ta_count)]
        first, parts, cube, table = lax.optimization_barrier((first, parts, cube, table))
        away = jnp.concatenate([x[: 2 * quarter] for x in parts], axis=0)
        tables = [(0, 2 * half), (1, 2 * half)]
        tables += [(k, 2 * quarter) for k in range(2, ta_count)]
        side_away, mate, found = lax.optimization_barrier(
            (
                swap(away, "pb", pb_count, 2),
                swap(jnp.concatenate([first[: 2 * half], away]), "pb", pb_count, 1),
                match(tables, (near, first, *parts)),
            )
        )
        side_mate = swap(side_away, "pb", pb_count, 1)
        pieces = (near, rest, first, away, side_away, mate, side_mate)
        made = full
    else:
        pieces = (
            lax.all_gather(qz_factor, "ta", axis=0, tiled=True),
            lax.all_gather(qy_factor, "ta", axis=0, tiled=True),
        )
        made = []
        shown = jnp.zeros((info_rows, rank), jnp.int32)
        shown = shown.at[0, :slots].set(table[:slots] + 1)
        shown = shown.at[1:3, :slots].set(table[slots:].reshape(2, slots))
        info = lax.all_gather(shown.astype(bf16), "ta", axis=0, tiled=True)
        found = match([(0, k * info_rows) for k in range(ta_count)], (info,))
    out = pl.pallas_call(
        functools.partial(term_kernel, edge, swaps),
        out_shape=[shape((ta_count * frames, rank), f32)] + made,
        in_specs=[smem_spec] + [vmem_spec] * (1 + len(pieces)),
        out_specs=[vmem_spec] * (1 + len(made)),
        compiler_params=params(16),
        name="terms",
    )(table, cube, *pieces)
    terms = out[0]
    if swaps:
        full_z, full_y = out[1:]
        arrived = jnp.concatenate(
            [
                swap(terms[k * frames : (k + 1) * frames], "ta", ta_count, k)
                for k in range(1, ta_count)
            ],
            axis=0,
        )
    else:
        full_z, full_y = pieces
        arrived = lax.all_to_all(terms, "ta", split_axis=0, concat_axis=0, tiled=True)
    square = [shape((rank, rank), f32)] + [shape((rank, rank), bf16)] * 5
    parts = pl.pallas_call(
        functools.partial(system_kernel, edge),
        out_shape=square,
        in_specs=[smem_spec] + [vmem_spec] * 2,
        out_specs=[vmem_spec] * 6,
        scratch_shapes=[pltpu.VMEM((rank, rank), f32)],
        compiler_params=params(16),
        name="system",
    )(found, full_z, full_y)
    kept, low = pl.pallas_call(
        functools.partial(solve_kernel, ta_count, swaps),
        out_shape=[shape((frames, rank), f32), shape((frames, rank), bf16)],
        in_specs=[vmem_spec] * 8,
        out_specs=[vmem_spec] * 2,
        scratch_shapes=[pltpu.VMEM((rank, rank), f32)],
        compiler_params=params(8),
        name="solve",
    )(terms, arrived, *parts)
    if swaps:
        others = jnp.concatenate([swap(low, "ta", ta_count, k) for k in range(1, ta_count)], axis=0)
    else:
        others = lax.all_gather(low, "ta", axis=0, tiled=True)
    misfit, new_rows = pl.pallas_call(
        functools.partial(misfit_kernel, ta_count, edge, swaps),
        out_shape=[shape((1, slots), f32), shape((frames, rank), f32)],
        in_specs=[smem_spec] + [vmem_spec] * 6,
        out_specs=[vmem_spec, hbm_spec],
        scratch_shapes=[
            pltpu.VMEM((ta_count, frames, rank), f32),
            pltpu.SemaphoreType.DMA,
        ],
        compiler_params=params(16),
        name="misfit",
    )(table, low, others, full_z, full_y, cube, kept)
    return (new_rows, misfit.reshape(1, 1, slots))


def solution(mesh):
    placed = (
        P(("series", "ta"), "pb", None, None, None, None),
        P(("series", "ta"), None),
        P(("series", "ta"), None),
        P(("series", "ta"), "pb", None),
        P(("series", "ta"), "pb", None, None),
    )

    return jax.shard_map(
        body,
        mesh=mesh,
        in_specs=placed,
        out_specs=(P(("series", "ta", "pb"), None), P(("series", "ta"), "pb", None)),
        check_vma=False,
    )
```
